128 devices in a mesh: pts: 128 (over z, y, x, core).
Axes of the slice: x: 4, y: 4, z: 4, core: 2. Of those that a mesh axis runs over, the one named last changes fastest.
Arguments:
- points: bfloat16 [65536, 1024], P('pts')
- weights: bfloat16 [65536, 512], P('pts'), may hold values from -2 to 2
- node_proj: bfloat16 [512, 65536], P(None, 'pts'), may hold values from -0.0625 to 0.0625
- skel_idx: int32 [128, 32], P('pts'), may hold values from 0 to 511, as said below
- near_list: int32 [128, 4], P('pts'), may hold values from 0 to 127, as said below
- near_count: int32 [128], P('pts'), may hold values from 1 to 4, as said below
- far_list: int32 [128, 4], P('pts'), may hold values from 0 to 7, as said below
- far_count: int32 [128], P('pts'), may hold values from 1 to 4
Outputs:
- potential: float32 [65536, 512], P('pts')
The draws below stay inside these ranges and needn't reach their ends.
Inputs may be any that keep to these rules, and one draw needn't show every extreme that they name: `skel_idx`: each row holds 32 distinct local point indices. `near_list`: row t lists distinct leaves among t - 2, t - 1, t + 1, t + 2 in its first near_count[t] slots; the other slots hold t. `near_count`: at most the number of leaves among t - 2 to t + 2 other than t. `far_list`: row t lists distinct nodes that hold none of the leaves t - 2 to t + 2 in its first far_count[t] slots; the other slots repeat the first entry.
All inputs are finite; a program needn't handle non-finite values.
Results may differ from the reference program's by a relative error of at most 0.003.
Values may be sent and summed in bfloat16 or wider, within the bound.
A program may use at most 128 MiB of HBM per device.

```python
import math
import jax
import jax.numpy as jnp
from jax import lax

DIM = 1024
WCOLS = 512
SKEL = 512
NODES = 8
NEAR = 4
FAR = 4
PTS_DEV = 512
GROUP = 16
SKL = 32
TOTAL = 65536
N_PTS = 128


def coord_scale(key):
    order = jax.random.permutation(jax.random.fold_in(key, 53), DIM)
    heavy = math.sqrt(0.5 * DIM / 16.0)
    light = math.sqrt(0.5 * DIM / (DIM - 16.0))
    scale = jnp.where(order < 16, jnp.float32(heavy), jnp.float32(light))
    return scale.astype(jnp.float32)[None, :]


def draw_points(key, part):
    keys = jax.random.split(key, 3)
    group = N_PTS // NODES
    scale = coord_scale(key)
    centres = jnp.clip(jax.random.normal(keys[0], (NODES, DIM), jnp.float32), -6.0, 6.0)
    offsets = jnp.clip(jax.random.normal(keys[1], (N_PTS, DIM), jnp.float32), -6.0, 6.0)
    noise = jnp.clip(jax.random.normal(keys[2], (PTS_DEV * N_PTS, DIM), jnp.float32), -6.0, 6.0)
    node_part = jnp.repeat(centres, group * PTS_DEV, axis=0)
    leaf_part = jnp.repeat(offsets * scale, PTS_DEV, axis=0)
    total = node_part + leaf_part + 1.2247 * noise * scale
    return total.astype(jnp.bfloat16)


def draw_skel_idx(key, part):
    keys = jax.random.split(jax.random.fold_in(key, 11), N_PTS)

    def pick(single):
        return jnp.sort(jax.random.permutation(single, PTS_DEV)[:SKL])
    return jax.vmap(pick)(keys).astype(jnp.int32)


def near_helper(key):
    base = jax.random.fold_in(key, 23)
    first, second = jax.random.split(base)
    leaf = jnp.arange(N_PTS, dtype=jnp.int32)[:, None]
    offsets = jnp.array([[-2, -1, 1, 2]], dtype=jnp.int32)
    cand = leaf + offsets
    valid = ((cand >= 0) & (cand < N_PTS)).astype(jnp.int32)
    noise = jax.random.randint(first, (N_PTS, 4), 0, 1 << 20)
    order = jnp.argsort(noise + (1 - valid) * (1 << 21), axis=1, stable=True)
    cand_sorted = jnp.take_along_axis(cand, order, axis=1)
    nvalid = jnp.sum(valid, axis=1)
    draw_count = jax.random.randint(second, (N_PTS,), 0, 1 << 20) % nvalid + 1
    count = jnp.where(leaf[:, 0] == 2, nvalid, draw_count).astype(jnp.int32)
    slots = jnp.arange(4, dtype=jnp.int32)[None, :]
    listed = jnp.where(slots < count[:, None], cand_sorted, leaf).astype(jnp.int32)
    return (listed, count)


def draw_near_list(key, part):
    return near_helper(key)[0]


def draw_near_count(key, part):
    return near_helper(key)[1]


def far_helper(key):
    base = jax.random.fold_in(key, 37)
    first, second = jax.random.split(base)
    leaf = jnp.arange(N_PTS, dtype=jnp.int32)
    group = N_PTS // NODES
    nodes = jnp.arange(NODES, dtype=jnp.int32)[None, :]
    excluded = jnp.zeros((N_PTS, NODES), jnp.int32)
    for offset in range(-2, 3):
        near_node = jnp.clip(leaf + offset, 0, N_PTS - 1) // group
        excluded = jnp.maximum(excluded, (near_node[:, None] == nodes).astype(jnp.int32))
    noise = jax.random.randint(first, (N_PTS, NODES), 0, 1 << 20)
    favoured = (leaf[:, None] == 0) & (nodes == NODES - 1)
    noise = jnp.where(favoured, -1, noise)
    order = jnp.argsort(noise + excluded * (1 << 21), axis=1, stable=True)[:, :FAR].astype(jnp.int32)
    draw_count = jax.random.randint(second, (N_PTS,), 0, 1 << 20) % FAR + 1
    count = jnp.where(leaf == 0, FAR, draw_count).astype(jnp.int32)
    slots = jnp.arange(FAR, dtype=jnp.int32)[None, :]
    listed = jnp.where(slots < count[:, None], order, order[:, :1]).astype(jnp.int32)
    return (listed, count)


def draw_far_list(key, part):
    return far_helper(key)[0]


def draw_far_count(key, part):
    return far_helper(key)[1]


def level_of(rng, dims, cuts, least, high):
    factor_of, own = 1.0, jax.random.fold_in(rng, 6)
    for dim, shards_of in cuts:
        draws = jnp.exp(jax.random.uniform(jax.random.fold_in(own, dim), (shards_of,), jnp.float32, least / len(cuts), high / len(cuts)))
        factor_of = factor_of * jnp.repeat(draws, dims[dim] // shards_of).reshape([-1 if axis == dim else 1 for axis in range(len(dims))])
    return factor_of


def centred(stream_key, extent, deviation, limit, shards=(), kind=jnp.bfloat16):
    values = deviation * jax.random.normal(stream_key, extent, jnp.float32)
    if shards:
        values = values * level_of(stream_key, extent, shards, -0.22, 0.18)
    return jnp.clip(values, -limit, limit).astype(kind)


def setup_inputs(seed: int = 0) -> dict:
    arg_keys = jax.random.split(jax.random.key(seed), 9)
    return {
        "points": draw_points(jax.random.fold_in(arg_keys[8], 71), 0),
        "weights": centred(arg_keys[1], (TOTAL, WCOLS), 0.15, 2.0, ((0, 128),)),
        "node_proj": centred(arg_keys[2], (SKEL, TOTAL), (PTS_DEV * GROUP) ** -0.5, 0.0625, ((1, 128),)),
        "skel_idx": draw_skel_idx(jax.random.fold_in(arg_keys[8], 71), 0),
        "near_list": draw_near_list(jax.random.fold_in(arg_keys[8], 71), 0),
        "near_count": draw_near_count(jax.random.fold_in(arg_keys[8], 71), 0),
        "far_list": draw_far_list(jax.random.fold_in(arg_keys[8], 71), 0),
        "far_count": draw_far_count(jax.random.fold_in(arg_keys[8], 71), 0),
    }


def kernel_sum(xpts, xsq, ypts, ysq, wts, gate):
    scores = lax.dot_general(xpts, ypts, (((1,), (1,)), ((), ())), preferred_element_type=jnp.float32)
    dist = xsq[:, None] + ysq[None, :] - 2.0 * scores
    kern = (jnp.exp(dist * (-0.5 / DIM)) * gate).astype(jnp.bfloat16)
    return jnp.dot(kern, wts, preferred_element_type=jnp.float32)


def reference(points, weights, node_proj, skel_idx, near_list, near_count, far_list, far_count):
    sq = jnp.sum(jnp.square(points.astype(jnp.float32)), axis=1)
    leaf_pts = points.reshape(N_PTS, PTS_DEV, DIM)
    leaf_sq = sq.reshape(N_PTS, PTS_DEV)
    leaf_w = weights.reshape(N_PTS, PTS_DEV, WCOLS)
    index = skel_idx.astype(jnp.int32)
    skel_pts = jnp.take_along_axis(leaf_pts, index[:, :, None], axis=1).reshape(NODES, SKEL, DIM)
    skel_sq = jnp.take_along_axis(leaf_sq, index, axis=1).reshape(NODES, SKEL)
    proj_leaf = jnp.transpose(node_proj.reshape(SKEL, N_PTS, PTS_DEV), (1, 0, 2))

    def partial_of(pair):
        return jnp.dot(pair[0], pair[1], preferred_element_type=jnp.float32)

    partials = lax.map(partial_of, (proj_leaf, leaf_w))
    group = N_PTS // NODES
    skel_w = jnp.sum(partials.reshape(NODES, group, SKEL, WCOLS), axis=1).astype(jnp.bfloat16)

    def one_leaf(target):
        xpts = leaf_pts[target]
        xsq = leaf_sq[target]
        total = kernel_sum(xpts, xsq, xpts, xsq, leaf_w[target], jnp.float32(1.0))
        for slot in range(NEAR):
            source = near_list[target, slot]
            gate = (slot < near_count[target]).astype(jnp.float32)
            total = total + kernel_sum(xpts, xsq, leaf_pts[source], leaf_sq[source], leaf_w[source], gate)
        for slot in range(FAR):
            node = far_list[target, slot]
            gate = (slot < far_count[target]).astype(jnp.float32)
            total = total + kernel_sum(xpts, xsq, skel_pts[node], skel_sq[node], skel_w[node], gate)
        return total

    result = lax.map(one_leaf, jnp.arange(N_PTS, dtype=jnp.int32))
    return result.reshape(N_PTS * PTS_DEV, WCOLS)
```

```python
import math

import jax
import jax.numpy as jnp
from jax import lax
from jax.experimental import pallas as pl
from jax.experimental.pallas import tpu as pltpu
from jax.sharding import PartitionSpec as P

F32, BF16 = jnp.float32, jnp.bfloat16
DIM = 1024
SIDE = 4
PTS = 512
COLS = 512
SKL = 32
NODES = 8
LANES = 128
UNIT = 16
SETROWS = SIDE * SKL
SOURCES = SETROWS * SIDE * SIDE
SCALE = math.log2(math.e) * 0.5 / DIM
OFF = -1e38
N_A = 4
NT = (((1,), (1,)), ((), ()))

UNITS = [(0, 0), (0, 1), (0, 3), (0, 2), (1, 2), (1, 3), (1, 1), (1, 0)]
UNIT_AT = {unit: place for place, unit in enumerate(UNITS)}


def body(*refs):
    (x_in, w_in, p_in, idx, near_list, near_count, far_list, far_count, out1, out2,
     xt, wt, pv, pf, ps, pr, ts, rr, fp, fw, nx, nw, kf, kn, acc, rs, rrecv, acol, ancol,
     cbo, cbp, cbn, cbf, gate, gatep, stage, lsem, ssem, rsem) = refs
    me = lax.axis_index("pts")
    core = lax.rem(me, 2)
    chip = me // 2
    x, y, z = lax.rem(chip, 4), lax.rem(chip // 4, 4), chip // 16
    sign = 2 * core - 1

    def dev(cx, cy, cz):
        return ((cz * 4 + cy) * 4 + cx) * 2 + core

    def plus(v, d):
        return lax.rem(v + d, 4)

    partner = me + 1 - 2 * core
    outer = lax.rem(me + sign + 128, 128)
    xs = {d: dev(plus(x, d), y, z) for d in (1, 3)}
    ys = {d: dev(x, plus(y, d), z) for d in (1, 3)}
    zs = {d: dev(x, y, plus(z, d)) for d in (1, 3)}
    ybase = y - lax.rem(y, 2)
    group = {}
    for ry in range(2):
        for rx in range(4):
            if rx or ry:
                cy = lax.rem(lax.rem(y, 2) + ry, 2)
                cx = plus(x, rx)
                group[(rx, ry)] = (dev(cx, ybase + cy, z), cy * 4 + cx)

    loads = []
    for k, (src, dst) in enumerate(((x_in, xt.at[pl.ds(0, PTS)]), (w_in, wt.at[pl.ds(0, PTS)]), (p_in, pv))):
        cp = pltpu.make_async_copy(src, dst, lsem.at[k])
        cp.start()
        loads.append(cp)

    barrier = pltpu.get_barrier_semaphore()
    peers = [d for d, _ in group.values()] + list(ys.values()) + list(zs.values()) + [partner, outer]
    for d in peers:
        pl.semaphore_signal(barrier, inc=1, device_id=(d,), device_id_type=pl.DeviceIdType.MESH)

    def any_of(ref, count, value):
        hit = (ref[0, 0] == value) & (count > 0)
        for s in range(1, 4):
            hit = hit | ((ref[0, s] == value) & (count > s))
        return hit

    fcount, ncount = far_count[0], near_count[0]
    for n in range(NODES):
        gate[n : n + 1, :] = jnp.full((1, LANES), jnp.where(any_of(far_list, fcount, n), 0.0, OFF), F32)
    for row, step, yes, no in ((8, 1, 0.0, OFF), (9, -1, 0.0, OFF), (10, 2, 1.0, 0.0), (11, -2, 0.0, OFF)):
        hit = any_of(near_list, ncount, me + sign * step)
        gate[row : row + 1, :] = jnp.full((1, LANES), jnp.where(hit, yes, no), F32)

    rowi = lax.broadcasted_iota(jnp.int32, (SKL, LANES), 0)
    lane = lax.broadcasted_iota(jnp.int32, (SKL, LANES), 1)
    col = jnp.zeros((SKL, LANES), jnp.int32)
    for r in range(SKL):
        col = jnp.where(rowi == r, idx[0, r], col)
    onehot = jnp.concatenate(
        [jnp.where(col == lane + LANES * j, 1.0, 0.0).astype(BF16) for j in range(PTS // LANES)], axis=1
    )
    loads[0].wait()
    skel = jnp.dot(onehot, xt[0:PTS, :], preferred_element_type=F32).astype(BF16)

    def at(dy, dz, unit):
        return (dz * 4 + dy) * SETROWS + unit * UNIT

    for h in range(2):
        fp[pl.ds(at(0, 0, UNIT_AT[(h, 0)]), UNIT), :] = skel[h * UNIT : (h + 1) * UNIT]

    pl.semaphore_wait(barrier, len(peers))

    sent = {}

    def send(key, src, dst, device):
        n = len(sent)
        cp = pltpu.make_async_remote_copy(
            src_ref=src, dst_ref=dst, send_sem=ssem.at[n], recv_sem=rsem.at[n],
            device_id=(device,), device_id_type=pl.DeviceIdType.MESH,
        )
        cp.start()
        sent[key] = cp

    def got(*key):
        sent[key].wait_recv()

    def rows_send(key, buf, device, src, dst, units):
        lo, hi = units
        if hi > lo:
            n = (hi - lo) * UNIT
            send(key, buf.at[pl.ds(at(*src, lo), n)], buf.at[pl.ds(at(*dst, lo), n)], device)

    BUF = {"p": fp, "w": fw}

    def x_own(t):
        for d in (1, 3):
            for h in range(2):
                u, v = UNIT_AT[(h, 0)], UNIT_AT[(h, (4 - d) % 4)]
                send((t, "x", d, h), BUF[t].at[pl.ds(at(0, 0, u), UNIT)], BUF[t].at[pl.ds(at(0, 0, v), UNIT)], xs[d])

    def x_fwd(t):
        for d, h in ((1, 0), (3, 1)):
            got(t, "x", d, h)
            u, v = UNIT_AT[(h, (4 - d) % 4)], UNIT_AT[(h, 2)]
            send((t, "xf", d), BUF[t].at[pl.ds(at(0, 0, u), UNIT)], BUF[t].at[pl.ds(at(0, 0, v), UNIT)], xs[d])
        for d, h in ((1, 1), (3, 0)):
            got(t, "x", d, h)

    def x_done(t):
        for d in (1, 3):
            got(t, "xf", d)

    A_ALL, B_ALL = (0, N_A), (N_A, 8)
    GROUPS_A = [(0, 1), (1, 3), (3, N_A)]
    GROUPS_B = [(7, 8), (5, 7), (N_A, 5)]

    def stage_one(t, ga, gb, tag):
        for d in (1, 3):
            rows_send((t, "A2", d, tag), BUF[t], ys[d], (0, 0), ((4 - d) % 4, 0), ga)
            rows_send((t, "B2", d, tag), BUF[t], zs[d], (0, 0), (0, (4 - d) % 4), gb)
        for d in (1, 3):
            rows_send((t, "A3", d, 0, tag), BUF[t], zs[d], (0, 0), (0, (4 - d) % 4), ga)
            rows_send((t, "B3", d, 0, tag), BUF[t], ys[d], (0, 0), ((4 - d) % 4, 0), gb)

    def wait_all(t, kind, d, *more):
        for key in list(sent):
            if key[:3] == (t, kind, d) and key[3 : 3 + len(more)] == more:
                got(*key)

    def cut(units, flip):
        lo, hi = units
        mid = lo + (hi - lo + (0 if flip else 1)) // 2
        return (lo, mid), (mid, hi)

    def leg_two(t):
        for d, part in ((1, 0), (3, 1)):
            s = (4 - d) % 4
            wait_all(t, "A2", d)
            rows_send((t, "A2f", d), BUF[t], ys[d], (s, 0), (2, 0), cut(A_ALL, False)[part])
            wait_all(t, "B2", d)
            rows_send((t, "B2f", d), BUF[t], zs[d], (0, s), (0, 2), cut(B_ALL, False)[part])
        for s in (3, 1):
            for d in (1, 3):
                rows_send((t, "A3", d, s), BUF[t], zs[d], (s, 0), (s, (4 - d) % 4), A_ALL)
                rows_send((t, "B3", d, s), BUF[t], ys[d], (0, s), ((4 - d) % 4, s), B_ALL)

    def leg_far(t):
        for d in (1, 3):
            wait_all(t, "A2f", d)
            wait_all(t, "B2f", d)
        for d in (1, 3):
            rows_send((t, "A3", d, 2), BUF[t], zs[d], (2, 0), (2, (4 - d) % 4), A_ALL)
            rows_send((t, "B3", d, 2), BUF[t], ys[d], (0, 2), ((4 - d) % 4, 2), B_ALL)

    def last_fwd(t, s):
        for d, part in ((1, 0), (3, 1)):
            e = (4 - d) % 4
            wait_all(t, "A3", d, s)
            rows_send((t, "A3f", d, s), BUF[t], zs[d], (s, e), (s, 2), cut(A_ALL, s % 2 == 1)[part])
            wait_all(t, "B3", d, s)
            rows_send((t, "B3f", d, s), BUF[t], ys[d], (e, s), (2, s), cut(B_ALL, s % 2 == 1)[part])

    def last_done(t, kind, s):
        for d in (1, 3):
            wait_all(t, kind, d, s)

    def sq_rows(ref, r0, out, o0, n):
        @pl.loop(0, n)
        def _(i):
            v = ref[pl.ds(pl.multiple_of(r0 + i * LANES, LANES), LANES), :].astype(F32)
            v = v * v
            t = v[:, 0:LANES]
            for j in range(1, DIM // LANES):
                t = t + v[:, j * LANES : (j + 1) * LANES]
            out[pl.ds(o0 + i, 1), :] = jnp.sum(t.T, axis=0, keepdims=True) * (-SCALE)

    def sq_cols(ref, r0, out, n):
        @pl.loop(0, n)
        def _(i):
            at_row = pl.multiple_of(r0 + i * LANES, LANES)
            v = ref[pl.ds(at_row, LANES), :].astype(F32)
            t = jnp.sum(v * v, axis=1, keepdims=True) * (-SCALE)
            out[pl.ds(at_row, LANES), :] = jnp.broadcast_to(t, (LANES, LANES))

    def kern_tile(xref, x0, colref, yref, y0, bias, kout, k0, n=PTS):
        s = lax.dot_general(xref[pl.ds(x0, PTS), :], yref[y0 : y0 + n, :], NT, preferred_element_type=F32)
        a = colref[pl.ds(x0, PTS), :]
        for j in range(n // LANES):
            e = s[:, j * LANES : (j + 1) * LANES] * (2.0 * SCALE) + (a + bias(j))
            kout[pl.ds(x0, PTS), k0 + j * LANES : k0 + (j + 1) * LANES] = jnp.exp2(e).astype(BF16)

    send(("x",), x_in, xt.at[pl.ds(PTS, PTS)], partner)
    x_own("p")
    stage_one("p", GROUPS_A[0], GROUPS_B[0], 0)
    send(("w",), w_in, wt.at[pl.ds(PTS, PTS)], partner)
    send(("g",), gate, gatep, partner)

    loads[1].wait()
    loads[2].wait()
    pf[...] = jnp.dot(pv[...], wt[0:PTS, :], preferred_element_type=F32)
    for j in range(NODES):
        ps[pl.ds(j * SKL, SKL), :] = pf[pl.ds(pl.multiple_of(64 * j + 32 * (1 - core), 32), SKL), :].astype(BF16)
    sq_rows(xt, 0, cbo, 0, 4)
    send(("ps",), ps, pr, partner)

    x_fwd("p")
    stage_one("p", GROUPS_A[1], GROUPS_B[1], 1)
    half = PTS // 2
    send(("nx", 0), x_in.at[pl.ds(0, half)], nx.at[pl.ds(0, half)], outer)
    sq_cols(xt, 0, acol, 4)

    got("ps")
    for j in range(NODES):
        mine = pf[pl.ds(pl.multiple_of(64 * j + 32 * core, 32), SKL), :] + pr[pl.ds(j * SKL, SKL), :].astype(F32)
        ts[pl.ds(j * SKL, SKL), :] = mine.astype(BF16)
    x_done("p")
    stage_one("p", GROUPS_A[2], GROUPS_B[2], 2)
    for (rx, ry), (device, j) in group.items():
        slot = ry * 4 + rx
        send(("rs", slot), ts.at[pl.ds(pl.multiple_of(j * SKL, SKL), SKL)], rr.at[pl.ds(slot * SKL, SKL)], device)

    def own_task(leaf):
        def bias(j):
            row = cbo[j : j + 1, :]
            return row if leaf == 0 else row + gatep[9:10, :]

        kern_tile(xt, leaf * PTS, acol, xt, 0, bias, kn, 0)
        rows = slice(leaf * PTS, (leaf + 1) * PTS)
        acc[rows, :] = jnp.dot(kn[rows, :], wt[0:PTS, :], preferred_element_type=F32)

    own_task(0)
    leg_two("p")

    own_row = pl.multiple_of((lax.rem(y, 2) * 4 + x) * 64 + 32 * core, 32)
    own_j = pl.multiple_of((lax.rem(y, 2) * 4 + x) * SKL, 32)
    block = pf[pl.ds(own_row, SKL), :] + pr[pl.ds(own_j, SKL), :].astype(F32)
    for slot in range(1, NODES):
        got("rs", slot)
        block = block + rr[pl.ds(slot * SKL, SKL), :].astype(F32)
    block = block.astype(BF16)
    for h in range(2):
        fw[pl.ds(at(0, 0, UNIT_AT[(h, 0)]), UNIT), :] = block[h * UNIT : (h + 1) * UNIT]
    got("x")
    sq_cols(xt, PTS, acol, 4)
    x_own("w")
    sq_rows(xt, PTS, cbp, 0, 4)
    last_fwd("p", 0)
    got("g")
    own_task(1)
    x_fwd("w")
    send(("nx", 1), x_in.at[pl.ds(half, half)], nx.at[pl.ds(half, half)], outer)
    send(("nw",), w_in, nw, outer)
    leg_far("p")
    x_done("w")
    stage_one("w", A_ALL, B_ALL, 0)
    last_fwd("p", 3)
    last_fwd("p", 1)

    def far_kern(g):
        sq_rows(fp, g * PTS, cbf, 4 * g, 4)
        for dy in range(4):
            node = plus(z, g) * 2 + plus(y, dy) // 2
            s = 4 * g + dy
            row = cbf[s : s + 1, :]
            stage[s : s + 1, :] = row + gate[pl.ds(node, 1), :]
            stage[16 + s : 17 + s, :] = row + gatep[pl.ds(node, 1), :]

        @pl.loop(0, 2)
        def _(leaf):
            def bias(j):
                return stage[pl.ds(leaf * 16 + 4 * g + j, 1), :]

            kern_tile(xt, pl.multiple_of(leaf * PTS, PTS), acol, fp, g * PTS, bias, kf, g * PTS)

    last_done("p", "B3f", 0)
    far_kern(0)
    leg_two("w")
    last_fwd("p", 2)
    last_fwd("w", 0)
    for s in (1, 3):
        last_done("p", "B3f", s)
    far_kern(3)
    leg_far("w")
    far_kern(1)
    last_fwd("w", 3)
    last_fwd("w", 1)
    last_done("p", "B3f", 2)
    for s in range(4):
        last_done("p", "A3f", s)
    far_kern(2)
    last_fwd("w", 2)

    got("nx", 0)
    got("nx", 1)
    got("nw")
    got("w")
    sq_rows(nx, 0, cbn, 0, 4)
    sq_cols(nx, 0, ancol, 4)
    kern_tile(nx, 0, ancol, xt, PTS, lambda j: cbp[j : j + 1, :], kn, 0)
    rs[...] = jnp.dot(kn[0:PTS, :], wt[PTS : 2 * PTS, :], preferred_element_type=F32).astype(BF16)
    for leaf, row, ref in ((0, 8, gate), (1, 11, gatep)):
        kern_tile(xt, leaf * PTS, acol, nx, 0, lambda j: cbn[j : j + 1, :] + ref[row : row + 1, :], kn, 0)
        if leaf == 0:
            send(("r",), rs, rrecv, outer)
        rows = slice(leaf * PTS, (leaf + 1) * PTS)
        acc[rows, :] += jnp.dot(kn[rows, :], nw[...], preferred_element_type=F32)

    def far_sum(g, leaf):
        rows = slice(leaf * PTS, (leaf + 1) * PTS)
        acc[rows, :] += jnp.dot(
            kf[rows, g * PTS : (g + 1) * PTS], fw[g * PTS : (g + 1) * PTS, :], preferred_element_type=F32
        )

    last_done("w", "B3f", 0)
    for leaf in (1, 0):
        far_sum(0, leaf)
    last_done("w", "B3f", 3)
    last_done("w", "B3f", 1)
    for g in (3, 1):
        for leaf in (1, 0):
            far_sum(g, leaf)
    last_done("w", "B3f", 2)
    for s in range(4):
        last_done("w", "A3f", s)
    for leaf in (1, 0):
        far_sum(2, leaf)

    send(("acc",), acc.at[pl.ds(PTS, PTS)], out2, partner)
    got("r")
    for j in range(COLS // LANES):
        c = slice(j * LANES, (j + 1) * LANES)
        acc[0:PTS, c] = acc[0:PTS, c] + rrecv[:, c].astype(F32) * gate[10:11, :]
    cp = pltpu.make_async_copy(acc.at[pl.ds(0, PTS)], out1, lsem.at[3])
    cp.start()
    got("acc")
    for copy in sent.values():
        copy.wait_send()
    cp.wait()


def shards(points, weights, node_proj, skel_idx, near_list, near_count, far_list, far_count):
    smem = pl.BlockSpec(memory_space=pltpu.SMEM)
    hbm = pl.BlockSpec(memory_space=pl.ANY)
    vm = pltpu.VMEM
    scratch = [
        vm((2 * PTS, DIM), BF16), vm((2 * PTS, COLS), BF16), vm((PTS, PTS), BF16), vm((PTS, COLS), F32),
        vm((NODES * SKL, COLS), BF16), vm((NODES * SKL, COLS), BF16), vm((NODES * SKL, COLS), BF16),
        vm((NODES * SKL, COLS), BF16),
        vm((SOURCES, DIM), BF16), vm((SOURCES, COLS), BF16), vm((PTS, DIM), BF16), vm((PTS, COLS), BF16),
        vm((2 * PTS, SOURCES), BF16), vm((2 * PTS, PTS), BF16), vm((2 * PTS, COLS), F32),
        vm((PTS, COLS), BF16), vm((PTS, COLS), BF16),
        vm((2 * PTS, LANES), F32), vm((PTS, LANES), F32),
        vm((8, LANES), F32), vm((8, LANES), F32), vm((8, LANES), F32), vm((16, LANES), F32),
        vm((16, LANES), F32), vm((16, LANES), F32), vm((32, LANES), F32),
        pltpu.SemaphoreType.DMA((4,)), pltpu.SemaphoreType.DMA((160,)), pltpu.SemaphoreType.DMA((160,)),
    ]
    mine, theirs = pl.pallas_call(
        body,
        out_shape=(jax.ShapeDtypeStruct((PTS, COLS), F32),) * 2,
        in_specs=[hbm] * 3 + [smem] * 5,
        out_specs=(hbm, hbm),
        scratch_shapes=scratch,
        compiler_params=pltpu.CompilerParams(collective_id=0, has_side_effects=True),
    )(points, weights, node_proj, skel_idx, near_list, near_count, far_list, far_count)
    return mine + theirs


def solution(mesh):
    in_specs = (
        P("pts", None), P("pts", None), P(None, "pts"), P("pts", None),
        P("pts", None), P("pts"), P("pts", None), P("pts"),
    )
    return jax.shard_map(shards, mesh=mesh, in_specs=in_specs, out_specs=P("pts", None), check_vma=False)
```

```python
import math

import jax
import jax.numpy as jnp
from jax import lax
from jax.experimental import pallas as pl
from jax.experimental.pallas import tpu as pltpu
from jax.sharding import PartitionSpec as P

F32, BF16 = jnp.float32, jnp.bfloat16
DIM = 1024
SIDE = 4
PTS = 512
COLS = 512
SKL = 32
NODES = 8
LANES = 128
UNIT = 16
SETROWS = SIDE * SKL
SOURCES = SETROWS * SIDE * SIDE
SCALE = math.log2(math.e) * 0.5 / DIM
OFF = -1e38
N_A = 5
PIECE = PTS // 4
NT = (((1,), (1,)), ((), ()))

UNITS = [(0, 0), (0, 1), (0, 3), (0, 2), (1, 2), (1, 3), (1, 1), (1, 0)]
UNIT_AT = {unit: place for place, unit in enumerate(UNITS)}


def body(*refs):
    (x_in, w_in, p_in, idx, near_list, near_count, far_list, far_count, out1, out2,
     xt, wt, pv, pf, ps, pr, ts, rr, fp, fw, nx, nw, kf, kn, acc, rs, rrecv, hx, hw, hr, acol, ancol,
     cbo, cbp, cbn, cbf, gate, gatep, stage, lsem, ssem, rsem) = refs
    me = lax.axis_index("pts")
    core = lax.rem(me, 2)
    chip = me // 2
    x, y, z = lax.rem(chip, 4), lax.rem(chip // 4, 4), chip // 16
    sign = 2 * core - 1

    def dev(cx, cy, cz):
        return ((cz * 4 + cy) * 4 + cx) * 2 + core

    def plus(v, d):
        return lax.rem(v + d, 4)

    partner = me + 1 - 2 * core
    xs = {d: dev(plus(x, d), y, z) for d in (1, 3)}
    xfree = jnp.where(core == 0, xs[1], xs[3])
    ys = {d: dev(x, plus(y, d), z) for d in (1, 3)}
    zs = {d: dev(x, y, plus(z, d)) for d in (1, 3)}
    both = jnp.logical_and
    no = jnp.logical_not
    edge = jnp.where(core == 1, 3, 0)
    ahead = {"x": jnp.where(core == 1, xs[1], xs[3]), "y": jnp.where(core == 1, ys[1], ys[3]),
             "z": jnp.where(core == 1, zs[1], zs[3])}
    across = {axis: device - sign for axis, device in ahead.items()}
    xe, ye, ze = x == edge, y == edge, z == edge
    xf, yf, zf = x == 3 - edge, y == 3 - edge, z == 3 - edge
    inner, row_end, plane_end = no(xe), both(xe, no(ye)), both(both(xe, ye), no(ze))
    has_outer = no(both(both(xe, ye), ze))
    ybase = y - lax.rem(y, 2)
    group = {}
    for ry in range(2):
        for rx in range(4):
            if rx or ry:
                cy = lax.rem(lax.rem(y, 2) + ry, 2)
                cx = plus(x, rx)
                group[(rx, ry)] = (dev(cx, ybase + cy, z), cy * 4 + cx)

    loads = []
    for k, (src, dst) in enumerate(((x_in, xt.at[pl.ds(0, PTS)]), (w_in, wt.at[pl.ds(0, PTS)]), (p_in, pv))):
        cp = pltpu.make_async_copy(src, dst, lsem.at[k])
        cp.start()
        loads.append(cp)

    barrier = pltpu.get_barrier_semaphore()
    peers = [d for d, _ in group.values()] + list(ys.values()) + list(zs.values()) + [partner] + list(across.values())
    for d in peers:
        pl.semaphore_signal(barrier, inc=1, device_id=(d,), device_id_type=pl.DeviceIdType.MESH)

    def any_of(ref, count, value):
        hit = (ref[0, 0] == value) & (count > 0)
        for s in range(1, 4):
            hit = hit | ((ref[0, s] == value) & (count > s))
        return hit

    fcount, ncount = far_count[0], near_count[0]
    for n in range(NODES):
        gate[n : n + 1, :] = jnp.full((1, LANES), jnp.where(any_of(far_list, fcount, n), 0.0, OFF), F32)
    for row, step, found, missing in ((8, 1, 0.0, OFF), (9, -1, 0.0, OFF), (10, 2, 1.0, 0.0), (11, -2, 0.0, OFF)):
        hit = any_of(near_list, ncount, me + sign * step)
        gate[row : row + 1, :] = jnp.full((1, LANES), jnp.where(hit, found, missing), F32)

    rowi = lax.broadcasted_iota(jnp.int32, (SKL, LANES), 0)
    lane = lax.broadcasted_iota(jnp.int32, (SKL, LANES), 1)
    col = jnp.zeros((SKL, LANES), jnp.int32)
    for r in range(SKL):
        col = jnp.where(rowi == r, idx[0, r], col)
    onehot = jnp.concatenate(
        [jnp.where(col == lane + LANES * j, 1.0, 0.0).astype(BF16) for j in range(PTS // LANES)], axis=1
    )
    loads[0].wait()
    skel = jnp.dot(onehot, xt[0:PTS, :], preferred_element_type=F32).astype(BF16)

    def at(dy, dz, unit):
        return (dz * 4 + dy) * SETROWS + unit * UNIT

    for h in range(2):
        fp[pl.ds(at(0, 0, UNIT_AT[(h, 0)]), UNIT), :] = skel[h * UNIT : (h + 1) * UNIT]

    pl.semaphore_wait(barrier, len(peers))

    sent, landing = {}, {}

    started = []

    def send(key, src, dst, device, when=None):
        if key not in landing:
            landing[key] = len(landing)
        cp = pltpu.make_async_remote_copy(
            src_ref=src, dst_ref=dst, send_sem=ssem.at[len(started)], recv_sem=rsem.at[landing[key]],
            device_id=(device,), device_id_type=pl.DeviceIdType.MESH,
        )
        if when is None:
            cp.start()
        else:
            pl.when(when)(cp.start)
        started.append((cp, when))
        sent[key] = cp

    def got(*key):
        sent[key].wait_recv()

    def rows_send(key, buf, device, src, dst, units):
        lo, hi = units
        if hi > lo:
            n = (hi - lo) * UNIT
            send(key, buf.at[pl.ds(at(*src, lo), n)], buf.at[pl.ds(at(*dst, lo), n)], device)

    BUF = {"p": fp, "w": fw}

    def x_own(t):
        for d in (1, 3):
            for h in range(2):
                u, v = UNIT_AT[(h, 0)], UNIT_AT[(h, (4 - d) % 4)]
                send((t, "x", d, h), BUF[t].at[pl.ds(at(0, 0, u), UNIT)], BUF[t].at[pl.ds(at(0, 0, v), UNIT)], xs[d])

    def unit_rows(h, dx):
        return pl.multiple_of(jnp.where(core == 0, UNIT_AT[(h, dx)], UNIT_AT[(h, (4 - dx) % 4)]) * UNIT, UNIT)

    def x_hop(key, t, h, src_dx, dst_dx):
        send(key, BUF[t].at[pl.ds(unit_rows(h, src_dx), UNIT)], BUF[t].at[pl.ds(unit_rows(h, dst_dx), UNIT)], xfree)

    def x_fwd(t):
        for d in (1, 3):
            for h in range(2):
                got(t, "x", d, h)
        for h in range(2):
            x_hop((t, "xf", h), t, h, 3, 2)

    def x_done(t):
        for h in range(2):
            got(t, "xf", h)

    def x_ring(t, step):
        for h in range(2):
            if step:
                got(t, "xr", step - 1, h)
            if step < 3:
                x_hop((t, "xr", step, h), t, h, (4 - step) % 4, 3 - step)

    A_ALL, B_ALL = (0, N_A), (N_A, 8)
    GROUPS_A = [(0, 1), (1, 3), (3, N_A)]
    GROUPS_B = [(7, 8), (max(5, N_A), 7), (N_A, max(5, N_A))]

    def piece(ref, k):
        return ref.at[pl.ds(k * PIECE, PIECE)]

    def halo_send(h, ref, pieces):
        for k in pieces:
            send((h, "in", k), piece(ref, k), piece(HALO[h], k), across["x"], inner)
            axis = "x" if k < 2 else "y"
            send((h, "hop", k), piece(ref, k), piece(HOPS[h], k), ahead[axis], row_end)
            axis, slot = (("x", 0), ("x", 1), ("y", 2), ("z", 8))[k]
            send((h, "hop", slot), piece(ref, k), piece(HOPS[h], slot), ahead[axis], plane_end)

    def hop_wait(h, slot, when):
        pl.when(when)(sent[(h, "hop", slot)].wait_recv)

    def hop_send(h, slot, key, axis, when):
        dst = piece(HALO[h], key[2]) if key[1] == "in" else piece(HOPS[h], key[2])
        send(key, piece(HOPS[h], slot), dst, (across if key[1] == "in" else ahead)[axis], when)

    def relay_x(h):
        by_row, by_plane = both(xf, no(ye)), both(both(xf, ye), no(ze))
        for k in (0, 1):
            hop_wait(h, k, by_row | by_plane)
            hop_send(h, k, (h, "in", k), "y", by_row)
        hop_send(h, 0, (h, "hop", 4), "y", by_plane)
        hop_send(h, 1, (h, "hop", 5), "z", by_plane)

    def relay_yz(h):
        by_row, by_plane, by_line = both(xe, no(yf)), both(both(xe, yf), no(ze)), both(both(xe, ye), no(zf))
        hop_wait(h, 2, by_row | by_plane)
        hop_send(h, 2, (h, "in", 2), "x", by_row)
        hop_send(h, 2, (h, "hop", 6), "z", by_plane)
        hop_wait(h, 3, by_row)
        hop_send(h, 3, (h, "in", 3), "x", by_row)
        hop_wait(h, 8, by_line)
        hop_send(h, 8, (h, "hop", 7), "y", by_line)

    def relay_last(h):
        for slot, k, axis, when in (
            (4, 0, "z", both(both(xf, yf), no(ze))),
            (5, 1, "y", both(both(xf, ye), no(zf))),
            (6, 2, "x", both(both(xe, yf), no(zf))),
            (7, 3, "x", both(both(xe, yf), no(zf))),
        ):
            hop_wait(h, slot, when)
            hop_send(h, slot, (h, "in", k), axis, when)

    def halo_got(h):
        for k in range(4):
            pl.when(has_outer)(sent[(h, "in", k)].wait_recv)

    HALO = {"x": nx, "w": nw, "r": rrecv}
    HOPS = {"x": hx, "w": hw, "r": hr}

    def stage_one(t, ga, gb, tag):
        for d in (1, 3):
            rows_send((t, "A2", d, tag), BUF[t], ys[d], (0, 0), ((4 - d) % 4, 0), ga)
            rows_send((t, "B2", d, tag), BUF[t], zs[d], (0, 0), (0, (4 - d) % 4), gb)
        for d in (1, 3):
            rows_send((t, "A3", d, 0, tag), BUF[t], zs[d], (0, 0), (0, (4 - d) % 4), ga)
            rows_send((t, "B3", d, 0, tag), BUF[t], ys[d], (0, 0), ((4 - d) % 4, 0), gb)

    def wait_all(t, kind, d, *more):
        for key in list(sent):
            if key[:3] == (t, kind, d) and key[3 : 3 + len(more)] == more:
                got(*key)

    def cut(units, flip):
        lo, hi = units
        mid = lo + (hi - lo + (0 if flip else 1)) // 2
        return (lo, mid), (mid, hi)

    def pass_on(key, t, axis, other, units):
        for part, (lo, hi) in enumerate(units):
            if hi <= lo:
                continue
            slot, d = ((3, 1), (1, 3))[part]
            if axis == "y":
                rows_send(key + (part,), BUF[t], ys[d], (slot, other), (2, other), (lo, hi))
            else:
                rows_send(key + (part,), BUF[t], zs[d], (other, slot), (other, 2), (lo, hi))

    def leg_two(t):
        for d in (1, 3):
            wait_all(t, "A2", d)
        pass_on((t, "A2f", 0), t, "y", 0, cut(A_ALL, False))
        for d in (1, 3):
            wait_all(t, "B2", d)
        pass_on((t, "B2f", 0), t, "z", 0, cut(B_ALL, False))
        for s in (3, 1):
            for d in (1, 3):
                rows_send((t, "A3", d, s), BUF[t], zs[d], (s, 0), (s, (4 - d) % 4), A_ALL)
                rows_send((t, "B3", d, s), BUF[t], ys[d], (0, s), ((4 - d) % 4, s), B_ALL)

    def leg_far(t):
        wait_all(t, "A2f", 0)
        wait_all(t, "B2f", 0)
        for d in (1, 3):
            rows_send((t, "A3", d, 2), BUF[t], zs[d], (2, 0), (2, (4 - d) % 4), A_ALL)
            rows_send((t, "B3", d, 2), BUF[t], ys[d], (0, 2), ((4 - d) % 4, 2), B_ALL)

    def last_fwd(t, s):
        for d in (1, 3):
            wait_all(t, "A3", d, s)
        pass_on((t, "A3f", s), t, "z", s, cut(A_ALL, s % 2 == 1))
        for d in (1, 3):
            wait_all(t, "B3", d, s)
        pass_on((t, "B3f", s), t, "y", s, cut(B_ALL, s % 2 == 1))

    def last_done(t, kind, s):
        wait_all(t, kind, s)

    def sq_rows(ref, r0, out, o0, n):
        @pl.loop(0, n)
        def _(i):
            v = ref[pl.ds(pl.multiple_of(r0 + i * LANES, LANES), LANES), :].astype(F32)
            v = v * v
            t = v[:, 0:LANES]
            for j in range(1, DIM // LANES):
                t = t + v[:, j * LANES : (j + 1) * LANES]
            out[pl.ds(o0 + i, 1), :] = jnp.sum(t.T, axis=0, keepdims=True) * (-SCALE)

    def sq_cols(ref, r0, out, n):
        @pl.loop(0, n)
        def _(i):
            at_row = pl.multiple_of(r0 + i * LANES, LANES)
            v = ref[pl.ds(at_row, LANES), :].astype(F32)
            t = jnp.sum(v * v, axis=1, keepdims=True) * (-SCALE)
            out[pl.ds(at_row, LANES), :] = jnp.broadcast_to(t, (LANES, LANES))

    def kern_tile(xref, x0, colref, yref, y0, bias, kout, k0, n=PTS):
        s = lax.dot_general(xref[pl.ds(x0, PTS), :], yref[y0 : y0 + n, :], NT, preferred_element_type=F32)
        a = colref[pl.ds(x0, PTS), :]
        for j in range(n // LANES):
            e = s[:, j * LANES : (j + 1) * LANES] * (2.0 * SCALE) + (a + bias(j))
            kout[pl.ds(x0, PTS), k0 + j * LANES : k0 + (j + 1) * LANES] = jnp.exp2(e).astype(BF16)

    x_own("p")
    stage_one("p", GROUPS_A[0], GROUPS_B[0], 0)
    send(("x",), x_in, xt.at[pl.ds(PTS, PTS)], partner)
    halo_send("x", x_in, (0, 1))
    send(("w",), w_in, wt.at[pl.ds(PTS, PTS)], partner)
    send(("g",), gate, gatep, partner)

    loads[1].wait()
    loads[2].wait()
    pf[...] = jnp.dot(pv[...], wt[0:PTS, :], preferred_element_type=F32)
    for j in range(NODES):
        ps[pl.ds(j * SKL, SKL), :] = pf[pl.ds(pl.multiple_of(64 * j + 32 * (1 - core), 32), SKL), :].astype(BF16)
    sq_rows(xt, 0, cbo, 0, 4)
    send(("ps",), ps, pr, partner)

    x_fwd("p")
    stage_one("p", GROUPS_A[1], GROUPS_B[1], 1)
    sq_cols(xt, 0, acol, 4)

    got("ps")
    for j in range(NODES):
        mine = pf[pl.ds(pl.multiple_of(64 * j + 32 * core, 32), SKL), :] + pr[pl.ds(j * SKL, SKL), :].astype(F32)
        ts[pl.ds(j * SKL, SKL), :] = mine.astype(BF16)
    x_done("p")
    stage_one("p", GROUPS_A[2], GROUPS_B[2], 2)
    for (rx, ry), (device, j) in group.items():
        slot = ry * 4 + rx
        send(("rs", slot), ts.at[pl.ds(pl.multiple_of(j * SKL, SKL), SKL)], rr.at[pl.ds(slot * SKL, SKL)], device)
    halo_send("x", x_in, (2, 3))

    def own_task(leaf):
        def bias(j):
            row = cbo[j : j + 1, :]
            return row if leaf == 0 else row + gatep[9:10, :]

        kern_tile(xt, leaf * PTS, acol, xt, 0, bias, kn, 0)
        rows = slice(leaf * PTS, (leaf + 1) * PTS)
        acc[rows, :] = jnp.dot(kn[rows, :], wt[0:PTS, :], preferred_element_type=F32)

    own_task(0)
    leg_two("p")
    relay_x("x")

    own_row = pl.multiple_of((lax.rem(y, 2) * 4 + x) * 64 + 32 * core, 32)
    own_j = pl.multiple_of((lax.rem(y, 2) * 4 + x) * SKL, 32)
    block = pf[pl.ds(own_row, SKL), :] + pr[pl.ds(own_j, SKL), :].astype(F32)
    for slot in range(1, NODES):
        got("rs", slot)
        block = block + rr[pl.ds(slot * SKL, SKL), :].astype(F32)
    block = block.astype(BF16)
    for h in range(2):
        fw[pl.ds(at(0, 0, UNIT_AT[(h, 0)]), UNIT), :] = block[h * UNIT : (h + 1) * UNIT]
    got("x")
    sq_cols(xt, PTS, acol, 4)
    x_ring("w", 0)
    sq_rows(xt, PTS, cbp, 0, 4)
    last_fwd("p", 0)
    x_ring("w", 1)
    halo_send("w", w_in, (0, 1, 2, 3))
    got("g")
    own_task(1)
    x_ring("w", 2)
    leg_far("p")
    relay_yz("x")
    x_ring("w", 3)
    stage_one("w", A_ALL, B_ALL, 0)
    last_fwd("p", 3)
    last_fwd("p", 1)
    relay_last("x")

    def far_kern(g):
        sq_rows(fp, g * PTS, cbf, 4 * g, 4)
        for dy in range(4):
            node = plus(z, g) * 2 + plus(y, dy) // 2
            s = 4 * g + dy
            row = cbf[s : s + 1, :]
            stage[s : s + 1, :] = row + gate[pl.ds(node, 1), :]
            stage[16 + s : 17 + s, :] = row + gatep[pl.ds(node, 1), :]

        @pl.loop(0, 2)
        def _(leaf):
            def bias(j):
                return stage[pl.ds(leaf * 16 + 4 * g + j, 1), :]

            kern_tile(xt, pl.multiple_of(leaf * PTS, PTS), acol, fp, g * PTS, bias, kf, g * PTS)

    relay_x("w")
    last_done("p", "B3f", 0)
    far_kern(0)
    leg_two("w")
    last_fwd("p", 2)
    relay_yz("w")
    last_fwd("w", 0)

    halo_got("x")
    got("w")

    @pl.when(has_outer)
    def _():
        sq_rows(nx, 0, cbn, 0, 4)
        sq_cols(nx, 0, ancol, 4)
        kern_tile(nx, 0, ancol, xt, PTS, lambda j: cbp[j : j + 1, :], kn, 0)
        rs[...] = jnp.dot(kn[0:PTS, :], wt[PTS : 2 * PTS, :], preferred_element_type=F32).astype(BF16)

    for s in (1, 3):
        last_done("p", "B3f", s)
    halo_send("r", rs, (0, 1, 2, 3))
    far_kern(3)
    leg_far("w")
    relay_last("w")
    relay_x("r")
    far_kern(1)
    last_fwd("w", 3)
    last_fwd("w", 1)
    relay_yz("r")
    last_done("p", "B3f", 2)
    for s in range(4):
        last_done("p", "A3f", s)
    far_kern(2)
    last_fwd("w", 2)
    relay_last("r")

    halo_got("w")

    @pl.when(has_outer)
    def _():
        for leaf, row, ref in ((0, 8, gate), (1, 11, gatep)):
            kern_tile(xt, leaf * PTS, acol, nx, 0, lambda j: cbn[j : j + 1, :] + ref[row : row + 1, :], kn, 0)
            rows = slice(leaf * PTS, (leaf + 1) * PTS)
            acc[rows, :] += jnp.dot(kn[rows, :], nw[...], preferred_element_type=F32)

    def far_sum(g, leaf):
        rows = slice(leaf * PTS, (leaf + 1) * PTS)
        acc[rows, :] += jnp.dot(
            kf[rows, g * PTS : (g + 1) * PTS], fw[g * PTS : (g + 1) * PTS, :], preferred_element_type=F32
        )

    last_done("w", "B3f", 0)
    for leaf in (1, 0):
        far_sum(0, leaf)
    last_done("w", "B3f", 3)
    last_done("w", "B3f", 1)
    for g in (3, 1):
        for leaf in (1, 0):
            far_sum(g, leaf)
    last_done("w", "B3f", 2)
    for s in range(4):
        last_done("w", "A3f", s)
    for leaf in (1, 0):
        far_sum(2, leaf)

    send(("acc",), acc.at[pl.ds(PTS, PTS)], out2, partner)
    halo_got("r")

    @pl.when(has_outer)
    def _():
        for j in range(COLS // LANES):
            c = slice(j * LANES, (j + 1) * LANES)
            acc[0:PTS, c] = acc[0:PTS, c] + rrecv[:, c].astype(F32) * gate[10:11, :]

    cp = pltpu.make_async_copy(acc.at[pl.ds(0, PTS)], out1, lsem.at[3])
    cp.start()
    got("acc")
    for copy, when in started:
        if when is None:
            copy.wait_send()
        else:
            pl.when(when)(copy.wait_send)
    cp.wait()


def shards(points, weights, node_proj, skel_idx, near_list, near_count, far_list, far_count):
    smem = pl.BlockSpec(memory_space=pltpu.SMEM)
    hbm = pl.BlockSpec(memory_space=pl.ANY)
    vm = pltpu.VMEM
    scratch = [
        vm((2 * PTS, DIM), BF16), vm((2 * PTS, COLS), BF16), vm((PTS, PTS), BF16), vm((PTS, COLS), F32),
        vm((NODES * SKL, COLS), BF16), vm((NODES * SKL, COLS), BF16), vm((NODES * SKL, COLS), BF16),
        vm((NODES * SKL, COLS), BF16),
        vm((SOURCES, DIM), BF16), vm((SOURCES, COLS), BF16), vm((PTS, DIM), BF16), vm((PTS, COLS), BF16),
        vm((2 * PTS, SOURCES), BF16), vm((2 * PTS, PTS), BF16), vm((2 * PTS, COLS), F32),
        vm((PTS, COLS), BF16), vm((PTS, COLS), BF16),
        vm((9 * PIECE, DIM), BF16), vm((9 * PIECE, COLS), BF16), vm((9 * PIECE, COLS), BF16),
        vm((2 * PTS, LANES), F32), vm((PTS, LANES), F32),
        vm((8, LANES), F32), vm((8, LANES), F32), vm((8, LANES), F32), vm((16, LANES), F32),
        vm((16, LANES), F32), vm((16, LANES), F32), vm((32, LANES), F32),
        pltpu.SemaphoreType.DMA((4,)), pltpu.SemaphoreType.DMA((240,)), pltpu.SemaphoreType.DMA((200,)),
    ]
    mine, theirs = pl.pallas_call(
        body,
        out_shape=(jax.ShapeDtypeStruct((PTS, COLS), F32),) * 2,
        in_specs=[hbm] * 3 + [smem] * 5,
        out_specs=(hbm, hbm),
        scratch_shapes=scratch,
        compiler_params=pltpu.CompilerParams(collective_id=0, has_side_effects=True),
    )(points, weights, node_proj, skel_idx, near_list, near_count, far_list, far_count)
    return mine + theirs


def solution(mesh):
    in_specs = (
        P("pts", None), P("pts", None), P(None, "pts"), P("pts", None),
        P("pts", None), P("pts"), P("pts", None), P("pts"),
    )
    return jax.shard_map(shards, mesh=mesh, in_specs=in_specs, out_specs=P("pts", None), check_vma=False)
```

```python
import math

import jax
import jax.numpy as jnp
from jax import lax
from jax.experimental import pallas as pl
from jax.experimental.pallas import tpu as pltpu
from jax.sharding import PartitionSpec as P

F32, BF16 = jnp.float32, jnp.bfloat16
DIM = 1024
SIDE = 4
PTS = 512
COLS = 512
SKL = 32
NODES = 8
LANES = 128
UNIT = 16
SETROWS = SIDE * SKL
SOURCES = SETROWS * SIDE * SIDE
SCALE = math.log2(math.e) * 0.5 / DIM
OFF = -1e38
N_A = {"p": 5, "w": 4}
PIECE = PTS // 4
NT = (((1,), (1,)), ((), ()))

UNITS = [(0, 0), (0, 1), (0, 3), (0, 2), (1, 2), (1, 3), (1, 1), (1, 0)]
UNIT_AT = {unit: place for place, unit in enumerate(UNITS)}


def body(*refs):
    (x_in, w_in, p_in, idx, near_list, near_count, far_list, far_count, out1, out2,
     xt, wt, pv, pf, ps, pr, ts, rr, fp, fw, nx, nw, kf, kn, acc, rs, rrecv, hx, hw, hr, early, late, acol, ancol,
     cbo, cbp, cbn, cbf, gate, gatep, stage, lsem, ssem, rsem) = refs
    me = lax.axis_index("pts")
    core = lax.rem(me, 2)
    chip = me // 2
    x, y, z = lax.rem(chip, 4), lax.rem(chip // 4, 4), chip // 16
    sign = 2 * core - 1

    def dev(cx, cy, cz):
        return ((cz * 4 + cy) * 4 + cx) * 2 + core

    def plus(v, d):
        return lax.rem(v + d, 4)

    partner = me + 1 - 2 * core
    xs = {d: dev(plus(x, d), y, z) for d in (1, 3)}
    xfree = jnp.where(core == 0, xs[1], xs[3])
    ys = {d: dev(x, plus(y, d), z) for d in (1, 3)}
    zs = {d: dev(x, y, plus(z, d)) for d in (1, 3)}
    both = jnp.logical_and
    no = jnp.logical_not
    edge = jnp.where(core == 1, 3, 0)
    ahead = {"x": jnp.where(core == 1, xs[1], xs[3]), "y": jnp.where(core == 1, ys[1], ys[3]),
             "z": jnp.where(core == 1, zs[1], zs[3])}
    across = {axis: device - sign for axis, device in ahead.items()}
    xe, ye, ze = x == edge, y == edge, z == edge
    xf, yf, zf = x == 3 - edge, y == 3 - edge, z == 3 - edge
    inner, row_end, plane_end = no(xe), both(xe, no(ye)), both(both(xe, ye), no(ze))
    has_outer = no(both(both(xe, ye), ze))
    ybase = y - lax.rem(y, 2)
    group = {}
    for ry in range(2):
        for rx in range(4):
            if rx or ry:
                cy = lax.rem(lax.rem(y, 2) + ry, 2)
                cx = plus(x, rx)
                group[(rx, ry)] = (dev(cx, ybase + cy, z), cy * 4 + cx)

    loads = []
    for k, (src, dst) in enumerate(((x_in, xt.at[pl.ds(0, PTS)]), (w_in, wt.at[pl.ds(0, PTS)]), (p_in, pv))):
        cp = pltpu.make_async_copy(src, dst, lsem.at[k])
        cp.start()
        loads.append(cp)

    barrier = pltpu.get_barrier_semaphore()
    peers = [d for d, _ in group.values()] + list(ys.values()) + list(zs.values()) + [partner] + list(across.values())
    for d in peers:
        pl.semaphore_signal(barrier, inc=1, device_id=(d,), device_id_type=pl.DeviceIdType.MESH)

    def any_of(ref, count, value):
        hit = (ref[0, 0] == value) & (count > 0)
        for s in range(1, 4):
            hit = hit | ((ref[0, s] == value) & (count > s))
        return hit

    fcount, ncount = far_count[0], near_count[0]
    for n in range(NODES):
        gate[n : n + 1, :] = jnp.full((1, LANES), jnp.where(any_of(far_list, fcount, n), 0.0, OFF), F32)
    for row, step, found, missing in ((8, 1, 0.0, OFF), (9, -1, 0.0, OFF), (10, 2, 1.0, 0.0), (11, -2, 0.0, OFF)):
        hit = any_of(near_list, ncount, me + sign * step)
        gate[row : row + 1, :] = jnp.full((1, LANES), jnp.where(hit, found, missing), F32)

    rowi = lax.broadcasted_iota(jnp.int32, (SKL, LANES), 0)
    lane = lax.broadcasted_iota(jnp.int32, (SKL, LANES), 1)
    col = jnp.zeros((SKL, LANES), jnp.int32)
    for r in range(SKL):
        col = jnp.where(rowi == r, idx[0, r], col)
    onehot = jnp.concatenate(
        [jnp.where(col == lane + LANES * j, 1.0, 0.0).astype(BF16) for j in range(PTS // LANES)], axis=1
    )
    loads[0].wait()
    skel = jnp.dot(onehot, xt[0:PTS, :], preferred_element_type=F32).astype(BF16)

    def at(dy, dz, unit):
        return (dz * 4 + dy) * SETROWS + unit * UNIT

    for h in range(2):
        fp[pl.ds(at(0, 0, UNIT_AT[(h, 0)]), UNIT), :] = skel[h * UNIT : (h + 1) * UNIT]

    pl.semaphore_wait(barrier, len(peers))

    sent, landing = {}, {}

    started = []

    def send(key, src, dst, device, when=None):
        if key not in landing:
            landing[key] = len(landing)
        cp = pltpu.make_async_remote_copy(
            src_ref=src, dst_ref=dst, send_sem=ssem.at[len(started)], recv_sem=rsem.at[landing[key]],
            device_id=(device,), device_id_type=pl.DeviceIdType.MESH,
        )
        if when is None:
            cp.start()
        else:
            pl.when(when)(cp.start)
        started.append((cp, when))
        sent[key] = cp

    def got(*key):
        sent[key].wait_recv()

    def rows_send(key, buf, device, src, dst, units):
        lo, hi = units
        if hi > lo:
            n = (hi - lo) * UNIT
            send(key, buf.at[pl.ds(at(*src, lo), n)], buf.at[pl.ds(at(*dst, lo), n)], device)

    BUF = {"p": fp, "w": fw}

    def x_own(t):
        for d in (1, 3):
            for h in range(2):
                u, v = UNIT_AT[(h, 0)], UNIT_AT[(h, (4 - d) % 4)]
                send((t, "x", d, h), BUF[t].at[pl.ds(at(0, 0, u), UNIT)], BUF[t].at[pl.ds(at(0, 0, v), UNIT)], xs[d])

    def unit_rows(h, dx):
        return pl.multiple_of(jnp.where(core == 0, UNIT_AT[(h, dx)], UNIT_AT[(h, (4 - dx) % 4)]) * UNIT, UNIT)

    def x_hop(key, t, h, src_dx, dst_dx):
        send(key, BUF[t].at[pl.ds(unit_rows(h, src_dx), UNIT)], BUF[t].at[pl.ds(unit_rows(h, dst_dx), UNIT)], xfree)

    def x_fwd(t):
        for d in (1, 3):
            for h in range(2):
                got(t, "x", d, h)
        for h in range(2):
            x_hop((t, "xf", h), t, h, 3, 2)

    def x_done(t):
        for h in range(2):
            got(t, "xf", h)

    def x_ring(t, step):
        for h in range(2):
            if step:
                got(t, "xr", step - 1, h)
            if step < 3:
                x_hop((t, "xr", step, h), t, h, (4 - step) % 4, 3 - step)

    A_ALL = {t: (0, n) for t, n in N_A.items()}
    B_ALL = {t: (n, 8) for t, n in N_A.items()}
    n_p = N_A["p"]
    GROUPS_A = [(0, 1), (1, 3), (3, n_p)]
    GROUPS_B = [(7, 8), (max(5, n_p), 7), (n_p, max(5, n_p))]

    def piece(ref, k):
        return ref.at[pl.ds(k * PIECE, PIECE)]

    def halo_send(h, ref, pieces):
        for k in pieces:
            send((h, "in", k), piece(ref, k), piece(HALO[h], k), across["x"], inner)
            axis = "x" if k < 2 else "y"
            send((h, "hop", k), piece(ref, k), piece(HOPS[h], k), ahead[axis], row_end)
            axis, slot = (("x", 0), ("x", 1), ("y", 2), ("z", 8))[k]
            send((h, "hop", slot), piece(ref, k), piece(HOPS[h], slot), ahead[axis], plane_end)

    def hop_wait(h, slot, when):
        pl.when(when)(sent[(h, "hop", slot)].wait_recv)

    def hop_send(h, slot, key, axis, when):
        dst = piece(HALO[h], key[2]) if key[1] == "in" else piece(HOPS[h], key[2])
        send(key, piece(HOPS[h], slot), dst, (across if key[1] == "in" else ahead)[axis], when)

    def relay_x(h):
        by_row, by_plane = both(xf, no(ye)), both(both(xf, ye), no(ze))
        for k in (0, 1):
            hop_wait(h, k, by_row | by_plane)
            hop_send(h, k, (h, "in", k), "y", by_row)
        hop_send(h, 0, (h, "hop", 4), "y", by_plane)
        hop_send(h, 1, (h, "hop", 5), "z", by_plane)

    def relay_yz(h):
        by_row, by_plane, by_line = both(xe, no(yf)), both(both(xe, yf), no(ze)), both(both(xe, ye), no(zf))
        hop_wait(h, 2, by_row | by_plane)
        hop_send(h, 2, (h, "in", 2), "x", by_row)
        hop_send(h, 2, (h, "hop", 6), "z", by_plane)
        hop_wait(h, 3, by_row)
        hop_send(h, 3, (h, "in", 3), "x", by_row)
        hop_wait(h, 8, by_line)
        hop_send(h, 8, (h, "hop", 7), "y", by_line)

    def relay_last(h):
        for slot, k, axis, when in (
            (4, 0, "z", both(both(xf, yf), no(ze))),
            (5, 1, "y", both(both(xf, ye), no(zf))),
            (6, 2, "x", both(both(xe, yf), no(zf))),
            (7, 3, "x", both(both(xe, yf), no(zf))),
        ):
            hop_wait(h, slot, when)
            hop_send(h, slot, (h, "in", k), axis, when)

    def halo_got(h):
        for k in range(4):
            pl.when(has_outer)(sent[(h, "in", k)].wait_recv)

    HALO = {"x": nx, "w": nw, "r": rrecv}
    HOPS = {"x": hx, "w": hw, "r": hr}

    def stage_one(t, ga, gb, tag):
        for d in (1, 3):
            rows_send((t, "A2", d, tag), BUF[t], ys[d], (0, 0), ((4 - d) % 4, 0), ga)
            rows_send((t, "B2", d, tag), BUF[t], zs[d], (0, 0), (0, (4 - d) % 4), gb)
        for d in (1, 3):
            rows_send((t, "A3", d, 0, tag), BUF[t], zs[d], (0, 0), (0, (4 - d) % 4), ga)
            rows_send((t, "B3", d, 0, tag), BUF[t], ys[d], (0, 0), ((4 - d) % 4, 0), gb)

    def wait_all(t, kind, d, *more):
        for key in list(sent):
            if key[:3] == (t, kind, d) and key[3 : 3 + len(more)] == more:
                got(*key)

    def cut(units, flip):
        lo, hi = units
        mid = lo + (hi - lo + (0 if flip else 1)) // 2
        return (lo, mid), (mid, hi)

    def pass_on(key, t, axis, other, units):
        for part, (lo, hi) in enumerate(units):
            if hi <= lo:
                continue
            slot, d = ((3, 1), (1, 3))[part]
            if axis == "y":
                rows_send(key + (part,), BUF[t], ys[d], (slot, other), (2, other), (lo, hi))
            else:
                rows_send(key + (part,), BUF[t], zs[d], (other, slot), (other, 2), (lo, hi))

    def leg_two(t):
        for d in (1, 3):
            wait_all(t, "A2", d)
        pass_on((t, "A2f", 0), t, "y", 0, cut(A_ALL[t], False))
        for d in (1, 3):
            wait_all(t, "B2", d)
        pass_on((t, "B2f", 0), t, "z", 0, cut(B_ALL[t], False))
        for s in (3, 1):
            for d in (1, 3):
                rows_send((t, "A3", d, s), BUF[t], zs[d], (s, 0), (s, (4 - d) % 4), A_ALL[t])
                rows_send((t, "B3", d, s), BUF[t], ys[d], (0, s), ((4 - d) % 4, s), B_ALL[t])

    def leg_far(t):
        wait_all(t, "A2f", 0)
        wait_all(t, "B2f", 0)
        for d in (1, 3):
            rows_send((t, "A3", d, 2), BUF[t], zs[d], (2, 0), (2, (4 - d) % 4), A_ALL[t])
            rows_send((t, "B3", d, 2), BUF[t], ys[d], (0, 2), ((4 - d) % 4, 2), B_ALL[t])

    def last_fwd(t, s):
        for d in (1, 3):
            wait_all(t, "A3", d, s)
        pass_on((t, "A3f", s), t, "z", s, cut(A_ALL[t], s % 2 == 1))
        for d in (1, 3):
            wait_all(t, "B3", d, s)
        pass_on((t, "B3f", s), t, "y", s, cut(B_ALL[t], s % 2 == 1))

    def last_done(t, kind, s):
        wait_all(t, kind, s)

    def sq_rows(ref, r0, out, o0, n):
        @pl.loop(0, n)
        def _(i):
            v = ref[pl.ds(pl.multiple_of(r0 + i * LANES, LANES), LANES), :].astype(F32)
            v = v * v
            t = v[:, 0:LANES]
            for j in range(1, DIM // LANES):
                t = t + v[:, j * LANES : (j + 1) * LANES]
            out[pl.ds(o0 + i, 1), :] = jnp.sum(t.T, axis=0, keepdims=True) * (-SCALE)

    def sq_cols(ref, r0, out, n):
        @pl.loop(0, n)
        def _(i):
            at_row = pl.multiple_of(r0 + i * LANES, LANES)
            v = ref[pl.ds(at_row, LANES), :].astype(F32)
            t = jnp.sum(v * v, axis=1, keepdims=True) * (-SCALE)
            out[pl.ds(at_row, LANES), :] = jnp.broadcast_to(t, (LANES, LANES))

    def kern_tile(xref, x0, colref, yref, y0, bias, kout, k0, n=PTS):
        s = lax.dot_general(xref[pl.ds(x0, PTS), :], yref[y0 : y0 + n, :], NT, preferred_element_type=F32)
        a = colref[pl.ds(x0, PTS), :]
        for j in range(n // LANES):
            e = s[:, j * LANES : (j + 1) * LANES] * (2.0 * SCALE) + (a + bias(j))
            kout[pl.ds(x0, PTS), k0 + j * LANES : k0 + (j + 1) * LANES] = jnp.exp2(e).astype(BF16)

    x_own("p")
    stage_one("p", GROUPS_A[0], GROUPS_B[0], 0)
    send(("x",), x_in, xt.at[pl.ds(PTS, PTS)], partner)
    halo_send("x", x_in, (0, 1))
    send(("w",), w_in, wt.at[pl.ds(PTS, PTS)], partner)
    send(("g",), gate, gatep, partner)

    loads[1].wait()
    loads[2].wait()
    pf[...] = jnp.dot(pv[...], wt[0:PTS, :], preferred_element_type=F32)
    for j in range(NODES):
        ps[pl.ds(j * SKL, SKL), :] = pf[pl.ds(pl.multiple_of(64 * j + 32 * (1 - core), 32), SKL), :].astype(BF16)
    sq_rows(xt, 0, cbo, 0, 4)
    send(("ps",), ps, pr, partner)

    x_fwd("p")
    stage_one("p", GROUPS_A[1], GROUPS_B[1], 1)
    sq_cols(xt, 0, acol, 4)

    got("ps")
    for j in range(NODES):
        mine = pf[pl.ds(pl.multiple_of(64 * j + 32 * core, 32), SKL), :] + pr[pl.ds(j * SKL, SKL), :].astype(F32)
        ts[pl.ds(j * SKL, SKL), :] = mine.astype(BF16)
    x_done("p")
    stage_one("p", GROUPS_A[2], GROUPS_B[2], 2)
    for (rx, ry), (device, j) in group.items():
        slot = ry * 4 + rx
        send(("rs", slot), ts.at[pl.ds(pl.multiple_of(j * SKL, SKL), SKL)], rr.at[pl.ds(slot * SKL, SKL)], device)
    halo_send("x", x_in, (2, 3))

    def own_task(leaf):
        def bias(j):
            row = cbo[j : j + 1, :]
            return row if leaf == 0 else row + gatep[9:10, :]

        kern_tile(xt, leaf * PTS, acol, xt, 0, bias, kn, 0)
        rows = slice(leaf * PTS, (leaf + 1) * PTS)
        acc[rows, :] = jnp.dot(kn[rows, :], wt[0:PTS, :], preferred_element_type=F32)

    own_task(0)
    leg_two("p")
    relay_x("x")

    own_row = pl.multiple_of((lax.rem(y, 2) * 4 + x) * 64 + 32 * core, 32)
    own_j = pl.multiple_of((lax.rem(y, 2) * 4 + x) * SKL, 32)
    block = pf[pl.ds(own_row, SKL), :] + pr[pl.ds(own_j, SKL), :].astype(F32)
    for slot in range(1, NODES):
        got("rs", slot)
        block = block + rr[pl.ds(slot * SKL, SKL), :].astype(F32)
    block = block.astype(BF16)
    for h in range(2):
        fw[pl.ds(at(0, 0, UNIT_AT[(h, 0)]), UNIT), :] = block[h * UNIT : (h + 1) * UNIT]
    got("x")
    sq_cols(xt, PTS, acol, 4)
    x_ring("w", 0)
    sq_rows(xt, PTS, cbp, 0, 4)
    last_fwd("p", 0)
    x_ring("w", 1)
    halo_send("w", w_in, (0, 1, 2, 3))
    got("g")
    own_task(1)
    x_ring("w", 2)
    leg_far("p")
    relay_yz("x")
    x_ring("w", 3)
    stage_one("w", A_ALL["w"], B_ALL["w"], 0)
    last_fwd("p", 3)
    last_fwd("p", 1)
    relay_last("x")

    def far_kern(g):
        sq_rows(fp, g * PTS, cbf, 4 * g, 4)
        for dy in range(4):
            node = plus(z, g) * 2 + plus(y, dy) // 2
            s = 4 * g + dy
            row = cbf[s : s + 1, :]
            stage[s : s + 1, :] = row + gate[pl.ds(node, 1), :]
            stage[16 + s : 17 + s, :] = row + gatep[pl.ds(node, 1), :]

        @pl.loop(0, 2)
        def _(leaf):
            def bias(j):
                return stage[pl.ds(leaf * 16 + 4 * g + j, 1), :]

            kern_tile(xt, pl.multiple_of(leaf * PTS, PTS), acol, fp, g * PTS, bias, kf, g * PTS)

    relay_x("w")
    last_done("p", "B3f", 0)
    far_kern(0)
    leg_two("w")
    last_fwd("p", 2)
    relay_yz("w")
    last_fwd("w", 0)

    halo_got("x")
    got("w")

    @pl.when(has_outer)
    def _():
        sq_rows(nx, 0, cbn, 0, 4)
        sq_cols(nx, 0, ancol, 4)
        kern_tile(nx, 0, ancol, xt, PTS, lambda j: cbp[j : j + 1, :], kn, 0)
        rs[...] = jnp.dot(kn[0:PTS, :], wt[PTS : 2 * PTS, :], preferred_element_type=F32).astype(BF16)

    for s in (1, 3):
        last_done("p", "B3f", s)
    halo_send("r", rs, (0, 1, 2, 3))
    far_kern(3)
    leg_far("w")
    relay_last("w")
    relay_x("r")
    far_kern(1)
    last_fwd("w", 3)
    last_fwd("w", 1)
    relay_yz("r")

    @pl.when(has_outer)
    def _():
        for leaf, row, ref in ((0, 8, gate), (1, 11, gatep)):
            kern_tile(xt, leaf * PTS, acol, nx, 0, lambda j: cbn[j : j + 1, :] + ref[row : row + 1, :], kn, 0)

    last_done("p", "B3f", 2)
    for s in range(4):
        last_done("p", "A3f", s)
    far_kern(2)
    last_fwd("w", 2)
    relay_last("r")

    def far_product(g, leaf):
        return jnp.dot(
            kf[leaf * PTS : (leaf + 1) * PTS, g * PTS : (g + 1) * PTS], fw[g * PTS : (g + 1) * PTS, :],
            preferred_element_type=F32,
        )

    def far_sum(g, leaf):
        acc[leaf * PTS : (leaf + 1) * PTS, :] += far_product(g, leaf)

    last_done("w", "B3f", 0)
    for leaf in (1, 0):
        far_sum(0, leaf)
    halo_got("w")

    @pl.when(has_outer)
    def _():
        for leaf in range(2):
            rows = slice(leaf * PTS, (leaf + 1) * PTS)
            acc[rows, :] += jnp.dot(kn[rows, :], nw[...], preferred_element_type=F32)

    last_done("w", "B3f", 3)
    last_done("w", "B3f", 1)
    for leaf in (1, 0):
        for g in (3, 1):
            far_sum(g, leaf)
    send(("acc",), acc.at[pl.ds(PTS, PTS)], early, partner)
    halo_got("r")

    @pl.when(has_outer)
    def _():
        for j in range(COLS // LANES):
            c = slice(j * LANES, (j + 1) * LANES)
            acc[0:PTS, c] = acc[0:PTS, c] + rrecv[:, c].astype(F32) * gate[10:11, :]

    last_done("w", "B3f", 2)
    for s in range(4):
        last_done("w", "A3f", s)
    late[...] = far_product(2, 1).astype(BF16)
    got("acc")
    acc[0:PTS, :] += early[...]
    send(("late",), late, out2, partner)
    out1[...] = acc[0:PTS, :] + far_product(2, 0)
    got("late")
    for copy, when in started:
        if when is None:
            copy.wait_send()
        else:
            pl.when(when)(copy.wait_send)


def shards(points, weights, node_proj, skel_idx, near_list, near_count, far_list, far_count):
    smem = pl.BlockSpec(memory_space=pltpu.SMEM)
    hbm = pl.BlockSpec(memory_space=pl.ANY)
    vm = pltpu.VMEM
    scratch = [
        vm((2 * PTS, DIM), BF16), vm((2 * PTS, COLS), BF16), vm((PTS, PTS), BF16), vm((PTS, COLS), F32),
        vm((NODES * SKL, COLS), BF16), vm((NODES * SKL, COLS), BF16), vm((NODES * SKL, COLS), BF16),
        vm((NODES * SKL, COLS), BF16),
        vm((SOURCES, DIM), BF16), vm((SOURCES, COLS), BF16), vm((PTS, DIM), BF16), vm((PTS, COLS), BF16),
        vm((2 * PTS, SOURCES), BF16), vm((2 * PTS, PTS), BF16), vm((2 * PTS, COLS), F32),
        vm((PTS, COLS), BF16), vm((PTS, COLS), BF16),
        vm((9 * PIECE, DIM), BF16), vm((9 * PIECE, COLS), BF16), vm((9 * PIECE, COLS), BF16),
        vm((PTS, COLS), F32), vm((PTS, COLS), BF16),
        vm((2 * PTS, LANES), F32), vm((PTS, LANES), F32),
        vm((8, LANES), F32), vm((8, LANES), F32), vm((8, LANES), F32), vm((16, LANES), F32),
        vm((16, LANES), F32), vm((16, LANES), F32), vm((32, LANES), F32),
        pltpu.SemaphoreType.DMA((4,)), pltpu.SemaphoreType.DMA((240,)), pltpu.SemaphoreType.DMA((200,)),
    ]
    mine, theirs = pl.pallas_call(
        body,
        out_shape=(pltpu.VMEM((PTS, COLS), F32), pltpu.VMEM((PTS, COLS), BF16)),
        in_specs=[hbm] * 3 + [smem] * 5,
        out_specs=(pl.BlockSpec(memory_space=pltpu.VMEM),) * 2,
        scratch_shapes=scratch,
        compiler_params=pltpu.CompilerParams(collective_id=0, has_side_effects=True),
    )(points, weights, node_proj, skel_idx, near_list, near_count, far_list, far_count)
    return mine + theirs.astype(F32)


def solution(mesh):
    in_specs = (
        P("pts", None), P("pts", None), P(None, "pts"), P("pts", None),
        P("pts", None), P("pts"), P("pts", None), P("pts"),
    )
    return jax.shard_map(shards, mesh=mesh, in_specs=in_specs, out_specs=P("pts", None), check_vma=False)
```

```python
import math

import jax
import jax.numpy as jnp
from jax import lax
from jax.experimental import pallas as pl
from jax.experimental.pallas import tpu as pltpu
from jax.sharding import PartitionSpec as P

F32, BF16 = jnp.float32, jnp.bfloat16
DIM = 1024
SIDE = 4
PTS = 512
COLS = 512
SKL = 32
NODES = 8
LANES = 128
UNIT = 16
SETROWS = SIDE * SKL
SOURCES = SETROWS * SIDE * SIDE
SCALE = math.log2(math.e) * 0.5 / DIM
OFF = -1e38
N_A = {"p": 5, "w": 5}
PIECE = PTS // 4
NT = (((1,), (1,)), ((), ()))

UNITS = [(0, 0), (0, 1), (0, 3), (0, 2), (1, 2), (1, 3), (1, 1), (1, 0)]
UNIT_AT = {unit: place for place, unit in enumerate(UNITS)}


def body(*refs):
    (x_in, w_in, p_in, idx_in, near_list_in, near_count_in, far_list_in, far_count_in, out1, out2,
     idx, near_list, near_count, far_list, far_count,
     xt, wt, pv, pf, ps, pr, ts, rr, fp, fw, nx, nw, kf, kn, acc, rs, rrecv, hx, hw, early, late, acol, ancol,
     cbo, cbp, cbn, cbf, gate, gatep, stage, lsem, ssem, rsem) = refs
    me = lax.axis_index("pts")
    core = lax.rem(me, 2)
    chip = me // 2
    x, y, z = lax.rem(chip, 4), lax.rem(chip // 4, 4), chip // 16
    sign = 2 * core - 1

    def dev(cx, cy, cz):
        return ((cz * 4 + cy) * 4 + cx) * 2 + core

    def plus(v, d):
        return lax.rem(v + d, 4)

    partner = me + 1 - 2 * core
    xs = {d: dev(plus(x, d), y, z) for d in (1, 3)}
    xfree = jnp.where(core == 0, xs[1], xs[3])
    ys = {d: dev(x, plus(y, d), z) for d in (1, 3)}
    zs = {d: dev(x, y, plus(z, d)) for d in (1, 3)}
    both = jnp.logical_and
    no = jnp.logical_not
    edge = jnp.where(core == 1, 3, 0)
    ahead = {"x": jnp.where(core == 1, xs[1], xs[3]), "y": jnp.where(core == 1, ys[1], ys[3]),
             "z": jnp.where(core == 1, zs[1], zs[3])}
    across = {axis: device - sign for axis, device in ahead.items()}
    xe, ye, ze = x == edge, y == edge, z == edge
    xf, yf, zf = x == 3 - edge, y == 3 - edge, z == 3 - edge
    inner, row_end, plane_end = no(xe), both(xe, no(ye)), both(both(xe, ye), no(ze))
    has_outer = no(both(both(xe, ye), ze))
    ybase = y - lax.rem(y, 2)
    group = {}
    for ry in range(2):
        for rx in range(4):
            if rx or ry:
                cy = lax.rem(lax.rem(y, 2) + ry, 2)
                cx = plus(x, rx)
                group[(rx, ry)] = (dev(cx, ybase + cy, z), cy * 4 + cx)

    loads = []
    for k, (src, dst) in enumerate(((x_in, xt.at[pl.ds(0, PTS)]), (w_in, wt.at[pl.ds(0, PTS)]), (p_in, pv))):
        cp = pltpu.make_async_copy(src, dst, lsem.at[k])
        cp.start()
        loads.append(cp)

    small = []
    for k, (src, dst) in enumerate(((idx_in, idx), (near_list_in, near_list), (near_count_in, near_count),
                                    (far_list_in, far_list), (far_count_in, far_count))):
        cp = pltpu.make_async_copy(src, dst, lsem.at[4 + k])
        cp.start()
        small.append(cp)

    barrier = pltpu.get_barrier_semaphore()
    peers = [d for d, _ in group.values()] + list(ys.values()) + list(zs.values()) + [partner] + list(across.values())
    for d in peers:
        pl.semaphore_signal(barrier, inc=1, device_id=(d,), device_id_type=pl.DeviceIdType.MESH)

    for cp in small:
        cp.wait()

    def any_of(ref, count, value):
        hit = (ref[0, 0] == value) & (count > 0)
        for s in range(1, 4):
            hit = hit | ((ref[0, s] == value) & (count > s))
        return hit

    fcount, ncount = far_count[0], near_count[0]
    for n in range(NODES):
        gate[n : n + 1, :] = jnp.full((1, LANES), jnp.where(any_of(far_list, fcount, n), 0.0, OFF), F32)
    for row, step, found, missing in ((8, 1, 0.0, OFF), (9, -1, 0.0, OFF), (10, 2, 1.0, 0.0), (11, -2, 0.0, OFF)):
        hit = any_of(near_list, ncount, me + sign * step)
        gate[row : row + 1, :] = jnp.full((1, LANES), jnp.where(hit, found, missing), F32)

    rowi = lax.broadcasted_iota(jnp.int32, (SKL, LANES), 0)
    lane = lax.broadcasted_iota(jnp.int32, (SKL, LANES), 1)
    col = jnp.zeros((SKL, LANES), jnp.int32)
    for r in range(SKL):
        col = jnp.where(rowi == r, idx[0, r], col)
    onehot = jnp.concatenate(
        [jnp.where(col == lane + LANES * j, 1.0, 0.0).astype(BF16) for j in range(PTS // LANES)], axis=1
    )
    loads[0].wait()
    skel = jnp.dot(onehot, xt[0:PTS, :], preferred_element_type=F32).astype(BF16)

    def at(dy, dz, unit):
        return (dz * 4 + dy) * SETROWS + unit * UNIT

    for h in range(2):
        fp[pl.ds(at(0, 0, UNIT_AT[(h, 0)]), UNIT), :] = skel[h * UNIT : (h + 1) * UNIT]

    pl.semaphore_wait(barrier, len(peers))

    sent, landing = {}, {}

    started = []

    def send(key, src, dst, device, when=None):
        if key not in landing:
            landing[key] = len(landing)
        cp = pltpu.make_async_remote_copy(
            src_ref=src, dst_ref=dst, send_sem=ssem.at[len(started)], recv_sem=rsem.at[landing[key]],
            device_id=(device,), device_id_type=pl.DeviceIdType.MESH,
        )
        if when is None:
            cp.start()
        else:
            pl.when(when)(cp.start)
        started.append((cp, when))
        sent[key] = cp

    def got(*key):
        sent[key].wait_recv()

    def rows_send(key, buf, device, src, dst, units):
        lo, hi = units
        if hi > lo:
            n = (hi - lo) * UNIT
            send(key, buf.at[pl.ds(at(*src, lo), n)], buf.at[pl.ds(at(*dst, lo), n)], device)

    BUF = {"p": fp, "w": fw}

    def x_own(t):
        for d in (1, 3):
            for h in range(2):
                u, v = UNIT_AT[(h, 0)], UNIT_AT[(h, (4 - d) % 4)]
                send((t, "x", d, h), BUF[t].at[pl.ds(at(0, 0, u), UNIT)], BUF[t].at[pl.ds(at(0, 0, v), UNIT)], xs[d])

    def unit_rows(h, dx):
        return pl.multiple_of(jnp.where(core == 0, UNIT_AT[(h, dx)], UNIT_AT[(h, (4 - dx) % 4)]) * UNIT, UNIT)

    def x_hop(key, t, h, src_dx, dst_dx):
        send(key, BUF[t].at[pl.ds(unit_rows(h, src_dx), UNIT)], BUF[t].at[pl.ds(unit_rows(h, dst_dx), UNIT)], xfree)

    def x_fwd(t):
        for d in (1, 3):
            for h in range(2):
                got(t, "x", d, h)
        for h in range(2):
            x_hop((t, "xf", h), t, h, 3, 2)

    def x_done(t):
        for h in range(2):
            got(t, "xf", h)

    def x_ring(t, step):
        for h in range(2):
            if step:
                got(t, "xr", step - 1, h)
            if step < 3:
                x_hop((t, "xr", step, h), t, h, (4 - step) % 4, 3 - step)

    A_ALL = {t: (0, n) for t, n in N_A.items()}
    B_ALL = {t: (n, 8) for t, n in N_A.items()}
    n_p = N_A["p"]
    GROUPS_A = [(0, 1), (1, 3), (3, n_p)]
    GROUPS_B = [(7, 8), (max(5, n_p), 7), (n_p, max(5, n_p))]

    def piece(ref, k):
        return ref.at[pl.ds(k * PIECE, PIECE)]

    def halo_send(h, ref, pieces):
        for k in pieces:
            send((h, "in", k), piece(ref, k), piece(HALO[h], k), across["x"], inner)
            axis = "x" if k < 2 else "y"
            send((h, "hop", k), piece(ref, k), piece(HOPS[h], k), ahead[axis], row_end)
            axis, slot = (("x", 0), ("x", 1), ("y", 2), ("z", 8))[k]
            send((h, "hop", slot), piece(ref, k), piece(HOPS[h], slot), ahead[axis], plane_end)

    def hop_wait(h, slot, when):
        pl.when(when)(sent[(h, "hop", slot)].wait_recv)

    def hop_send(h, slot, key, axis, when):
        dst = piece(HALO[h], key[2]) if key[1] == "in" else piece(HOPS[h], key[2])
        send(key, piece(HOPS[h], slot), dst, (across if key[1] == "in" else ahead)[axis], when)

    def relay_x(h):
        by_row, by_plane = both(xf, no(ye)), both(both(xf, ye), no(ze))
        for k in (0, 1):
            hop_wait(h, k, by_row | by_plane)
            hop_send(h, k, (h, "in", k), "y", by_row)
        hop_send(h, 0, (h, "hop", 4), "y", by_plane)
        hop_send(h, 1, (h, "hop", 5), "z", by_plane)

    def relay_yz(h):
        by_row, by_plane, by_line = both(xe, no(yf)), both(both(xe, yf), no(ze)), both(both(xe, ye), no(zf))
        hop_wait(h, 2, by_row | by_plane)
        hop_send(h, 2, (h, "in", 2), "x", by_row)
        hop_send(h, 2, (h, "hop", 6), "z", by_plane)
        hop_wait(h, 3, by_row)
        hop_send(h, 3, (h, "in", 3), "x", by_row)
        hop_wait(h, 8, by_line)
        hop_send(h, 8, (h, "hop", 7), "y", by_line)

    def relay_last(h):
        for slot, k, axis, when in (
            (4, 0, "z", both(both(xf, yf), no(ze))),
            (5, 1, "y", both(both(xf, ye), no(zf))),
            (6, 2, "x", both(both(xe, yf), no(zf))),
            (7, 3, "x", both(both(xe, yf), no(zf))),
        ):
            hop_wait(h, slot, when)
            hop_send(h, slot, (h, "in", k), axis, when)

    def halo_got(h):
        for k in range(4):
            pl.when(has_outer)(sent[(h, "in", k)].wait_recv)

    HALO = {"x": nx, "w": nw}
    HOPS = {"x": hx, "w": hw}

    y_even = lax.rem(y, 2) == 0
    y_far, y_pair = jnp.where(y_even, ys[3], ys[1]), jnp.where(y_even, ys[1], ys[3])
    y_seen, y_from = jnp.where(y_even, 1, 3), jnp.where(y_even, 3, 1)
    near_base = jnp.where(y_even, 2, 1)
    near_rows = pl.multiple_of(near_base * SETROWS, SETROWS)

    def pass_same(key, t, device, src, dst, units):
        lo, hi = units
        if hi > lo:
            n = (hi - lo) * UNIT
            src, dst = (
                pl.multiple_of(slot * SETROWS + lo * UNIT, UNIT) if not isinstance(slot, int) else slot * SETROWS + lo * UNIT
                for slot in (src, dst)
            )
            send(key, BUF[t].at[pl.ds(src, n)], BUF[t].at[pl.ds(dst, n)], device)

    def stage_one(t, ga, gb, tag):
        for d in (1, 3):
            rows_send((t, "A2", d, tag), BUF[t], ys[d], (0, 0), ((4 - d) % 4, 0), ga)
            rows_send((t, "B2", d, tag), BUF[t], zs[d], (0, 0), (0, (4 - d) % 4), gb)
        for d in (1, 3):
            rows_send((t, "A3", d, 0, tag), BUF[t], zs[d], (0, 0), (0, (4 - d) % 4), ga)
        pass_same((t, "B0", 0, tag), t, y_far, 0, y_seen, gb)

    def wait_all(t, kind, d, *more):
        for key in list(sent):
            if key[:3] == (t, kind, d) and key[3 : 3 + len(more)] == more:
                got(*key)

    def cut(units, flip):
        lo, hi = units
        mid = lo + (hi - lo + (0 if flip else 1)) // 2
        return (lo, mid), (mid, hi)

    def pass_on(key, t, axis, other, units):
        for part, (lo, hi) in enumerate(units):
            if hi <= lo:
                continue
            slot, d = ((3, 1), (1, 3))[part]
            if axis == "y":
                rows_send(key + (part,), BUF[t], ys[d], (slot, other), (2, other), (lo, hi))
            else:
                rows_send(key + (part,), BUF[t], zs[d], (other, slot), (other, 2), (lo, hi))

    def leg_two(t):
        for d in (1, 3):
            wait_all(t, "A2", d)
        pass_on((t, "A2f", 0), t, "y", 0, cut(A_ALL[t], False))
        for d in (1, 3):
            wait_all(t, "B2", d)
        pass_on((t, "B2f", 0), t, "z", 0, cut(B_ALL[t], False))
        for s in (3, 1):
            for d in (1, 3):
                rows_send((t, "A3", d, s), BUF[t], zs[d], (s, 0), (s, (4 - d) % 4), A_ALL[t])
                rows_send((t, "B3", d, s), BUF[t], ys[d], (0, s), ((4 - d) % 4, s), B_ALL[t])

    def leg_far(t):
        wait_all(t, "A2f", 0)
        wait_all(t, "B2f", 0)
        for d in (1, 3):
            rows_send((t, "A3", d, 2), BUF[t], zs[d], (2, 0), (2, (4 - d) % 4), A_ALL[t])
            rows_send((t, "B3", d, 2), BUF[t], ys[d], (0, 2), ((4 - d) % 4, 2), B_ALL[t])

    def last_fwd(t, s):
        for d in (1, 3):
            wait_all(t, "A3", d, s)
        pass_on((t, "A3f", s), t, "z", s, cut(A_ALL[t], s % 2 == 1))
        if s == 0:
            wait_all(t, "B0", 0)
            pass_same((t, "B3f", 0, 0), t, y_pair, y_from, 2, B_ALL[t])
            return
        for d in (1, 3):
            wait_all(t, "B3", d, s)
        pass_on((t, "B3f", s), t, "y", s, cut(B_ALL[t], s % 2 == 1))

    def last_done(t, kind, s):
        wait_all(t, kind, s)

    def sq_rows(ref, r0, out, o0, n):
        @pl.loop(0, n)
        def _(i):
            v = ref[pl.ds(pl.multiple_of(r0 + i * LANES, LANES), LANES), :].astype(F32)
            v = v * v
            t = v[:, 0:LANES]
            for j in range(1, DIM // LANES):
                t = t + v[:, j * LANES : (j + 1) * LANES]
            out[pl.ds(o0 + i, 1), :] = jnp.sum(t.T, axis=0, keepdims=True) * (-SCALE)

    def sq_cols(ref, r0, out, n):
        @pl.loop(0, n)
        def _(i):
            at_row = pl.multiple_of(r0 + i * LANES, LANES)
            v = ref[pl.ds(at_row, LANES), :].astype(F32)
            t = jnp.sum(v * v, axis=1, keepdims=True) * (-SCALE)
            out[pl.ds(at_row, LANES), :] = jnp.broadcast_to(t, (LANES, LANES))

    def kern_tile(xref, x0, colref, yref, y0, bias, kout, k0, n=PTS):
        s = lax.dot_general(xref[pl.ds(x0, PTS), :], yref[pl.ds(y0, n), :], NT, preferred_element_type=F32)
        a = colref[pl.ds(x0, PTS), :]
        for j in range(n // LANES):
            e = s[:, j * LANES : (j + 1) * LANES] * (2.0 * SCALE) + (a + bias(j))
            kout[pl.ds(x0, PTS), k0 + j * LANES : k0 + (j + 1) * LANES] = jnp.exp2(e).astype(BF16)

    x_own("p")
    stage_one("p", GROUPS_A[0], GROUPS_B[0], 0)
    send(("x",), x_in, xt.at[pl.ds(PTS, PTS)], partner)
    halo_send("x", x_in, (0, 1))
    send(("w",), w_in, wt.at[pl.ds(PTS, PTS)], partner)
    send(("g",), gate, gatep, partner)

    loads[1].wait()
    loads[2].wait()
    pf[...] = jnp.dot(pv[...], wt[0:PTS, :], preferred_element_type=F32)
    for j in range(NODES):
        ps[pl.ds(j * SKL, SKL), :] = pf[pl.ds(pl.multiple_of(64 * j + 32 * (1 - core), 32), SKL), :].astype(BF16)
    sq_rows(xt, 0, cbo, 0, 4)
    send(("ps",), ps, pr, partner)

    x_fwd("p")
    stage_one("p", GROUPS_A[1], GROUPS_B[1], 1)
    sq_cols(xt, 0, acol, 4)

    got("ps")
    for j in range(NODES):
        mine = pf[pl.ds(pl.multiple_of(64 * j + 32 * core, 32), SKL), :] + pr[pl.ds(j * SKL, SKL), :].astype(F32)
        ts[pl.ds(j * SKL, SKL), :] = mine.astype(BF16)
    x_done("p")
    stage_one("p", GROUPS_A[2], GROUPS_B[2], 2)
    for (rx, ry), (device, j) in group.items():
        slot = ry * 4 + rx
        send(("rs", slot), ts.at[pl.ds(pl.multiple_of(j * SKL, SKL), SKL)], rr.at[pl.ds(slot * SKL, SKL)], device)
    halo_send("x", x_in, (2, 3))

    def own_task(leaf):
        def bias(j):
            row = cbo[j : j + 1, :]
            return row if leaf == 0 else row + gatep[9:10, :]

        kern_tile(xt, leaf * PTS, acol, xt, 0, bias, kn, 0)
        rows = slice(leaf * PTS, (leaf + 1) * PTS)
        acc[rows, :] = jnp.dot(kn[rows, :], wt[0:PTS, :], preferred_element_type=F32)

    own_task(0)
    leg_two("p")
    relay_x("x")

    own_row = pl.multiple_of((lax.rem(y, 2) * 4 + x) * 64 + 32 * core, 32)
    own_j = pl.multiple_of((lax.rem(y, 2) * 4 + x) * SKL, 32)
    block = pf[pl.ds(own_row, SKL), :] + pr[pl.ds(own_j, SKL), :].astype(F32)
    for slot in range(1, NODES):
        got("rs", slot)
        block = block + rr[pl.ds(slot * SKL, SKL), :].astype(F32)
    block = block.astype(BF16)
    for h in range(2):
        fw[pl.ds(at(0, 0, UNIT_AT[(h, 0)]), UNIT), :] = block[h * UNIT : (h + 1) * UNIT]
    got("x")
    sq_cols(xt, PTS, acol, 4)
    x_ring("w", 0)
    sq_rows(xt, PTS, cbp, 0, 4)
    last_fwd("p", 0)
    x_ring("w", 1)
    halo_send("w", w_in, (0, 1, 2, 3))
    got("g")
    own_task(1)
    x_ring("w", 2)
    leg_far("p")
    relay_yz("x")
    x_ring("w", 3)
    stage_one("w", A_ALL["w"], B_ALL["w"], 0)
    last_fwd("p", 3)
    last_fwd("p", 1)
    relay_last("x")

    def far_kern(g):
        sets, first, base = (4, g * PTS, 0) if g else (2, near_rows, near_base)
        sq_rows(fp, first, cbf, 4 * g, sets)
        for dy in range(sets):
            node = plus(z, g) * 2 + plus(y, base + dy) // 2
            s = 4 * g + dy
            row = cbf[s : s + 1, :]
            stage[s : s + 1, :] = row + gate[pl.ds(node, 1), :]
            stage[16 + s : 17 + s, :] = row + gatep[pl.ds(node, 1), :]

        @pl.loop(0, 2)
        def _(leaf):
            def bias(j):
                return stage[pl.ds(leaf * 16 + 4 * g + j, 1), :]

            kern_tile(xt, pl.multiple_of(leaf * PTS, PTS), acol, fp, first, bias, kf, g * PTS, sets * SETROWS)

    relay_x("w")
    last_done("p", "B3f", 0)
    far_kern(0)
    leg_two("w")
    last_fwd("p", 2)
    relay_yz("w")
    last_fwd("w", 0)

    halo_got("x")
    got("w")

    @pl.when(has_outer)
    def _():
        sq_rows(nx, 0, cbn, 0, 4)
        sq_cols(nx, 0, ancol, 4)
        kern_tile(nx, 0, ancol, xt, PTS, lambda j: cbp[j : j + 1, :], kn, 0)
        rs[...] = jnp.dot(kn[0:PTS, :], wt[PTS : 2 * PTS, :], preferred_element_type=F32).astype(BF16)

    send(("r",), rs, rrecv, jnp.where(has_outer, me + sign, me), has_outer)

    for s in (1, 3):
        last_done("p", "B3f", s)
    far_kern(3)
    leg_far("w")
    relay_last("w")
    far_kern(1)
    last_fwd("w", 3)
    last_fwd("w", 1)

    @pl.when(has_outer)
    def _():
        for leaf, row, ref in ((0, 8, gate), (1, 11, gatep)):
            kern_tile(xt, leaf * PTS, acol, nx, 0, lambda j: cbn[j : j + 1, :] + ref[row : row + 1, :], kn, 0)

    last_done("p", "B3f", 2)
    for s in range(4):
        last_done("p", "A3f", s)
    far_kern(2)
    last_fwd("w", 2)

    def far_product(g, leaf):
        first, n = (g * PTS, PTS) if g else (near_rows, 2 * SETROWS)
        return jnp.dot(
            kf[leaf * PTS : (leaf + 1) * PTS, g * PTS : g * PTS + n], fw[pl.ds(first, n), :],
            preferred_element_type=F32,
        )

    def far_sum(g, leaf):
        acc[leaf * PTS : (leaf + 1) * PTS, :] += far_product(g, leaf)

    last_done("w", "B3f", 0)
    for leaf in (1, 0):
        far_sum(0, leaf)
    halo_got("w")

    @pl.when(has_outer)
    def _():
        for leaf in range(2):
            rows = slice(leaf * PTS, (leaf + 1) * PTS)
            acc[rows, :] += jnp.dot(kn[rows, :], nw[...], preferred_element_type=F32)

    last_done("w", "B3f", 3)
    last_done("w", "B3f", 1)
    for leaf in (1, 0):
        for g in (3, 1):
            far_sum(g, leaf)
    send(("acc",), acc.at[pl.ds(PTS, PTS)], early, partner)

    @pl.when(has_outer)
    def _():
        got("r")
        for j in range(COLS // LANES):
            c = slice(j * LANES, (j + 1) * LANES)
            acc[0:PTS, c] = acc[0:PTS, c] + rrecv[:, c].astype(F32) * gate[10:11, :]

    last_done("w", "B3f", 2)
    for s in range(4):
        last_done("w", "A3f", s)
    late[...] = far_product(2, 1).astype(BF16)
    got("acc")
    acc[0:PTS, :] += early[...]
    send(("late",), late, out2, partner)
    out1[...] = acc[0:PTS, :] + far_product(2, 0)
    got("late")
    for copy, when in started:
        if when is None:
            copy.wait_send()
        else:
            pl.when(when)(copy.wait_send)


def shards(points, weights, node_proj, skel_idx, near_list, near_count, far_list, far_count):
    hbm = pl.BlockSpec(memory_space=pl.ANY)
    vm = pltpu.VMEM
    words = [pltpu.SMEM(a.shape, a.dtype) for a in (skel_idx, near_list, near_count, far_list, far_count)]
    scratch = words + [
        vm((2 * PTS, DIM), BF16), vm((2 * PTS, COLS), BF16), vm((PTS, PTS), BF16), vm((PTS, COLS), F32),
        vm((NODES * SKL, COLS), BF16), vm((NODES * SKL, COLS), BF16), vm((NODES * SKL, COLS), BF16),
        vm((NODES * SKL, COLS), BF16),
        vm((SOURCES, DIM), BF16), vm((SOURCES, COLS), BF16), vm((PTS, DIM), BF16), vm((PTS, COLS), BF16),
        vm((2 * PTS, SOURCES), BF16), vm((2 * PTS, PTS), BF16), vm((2 * PTS, COLS), F32),
        vm((PTS, COLS), BF16), vm((PTS, COLS), BF16),
        vm((9 * PIECE, DIM), BF16), vm((9 * PIECE, COLS), BF16),
        vm((PTS, COLS), F32), vm((PTS, COLS), BF16),
        vm((2 * PTS, LANES), F32), vm((PTS, LANES), F32),
        vm((8, LANES), F32), vm((8, LANES), F32), vm((8, LANES), F32), vm((16, LANES), F32),
        vm((16, LANES), F32), vm((16, LANES), F32), vm((32, LANES), F32),
        pltpu.SemaphoreType.DMA((9,)), pltpu.SemaphoreType.DMA((240,)), pltpu.SemaphoreType.DMA((200,)),
    ]
    mine, theirs = pl.pallas_call(
        body,
        out_shape=(pltpu.VMEM((PTS, COLS), F32), pltpu.VMEM((PTS, COLS), BF16)),
        in_specs=[hbm] * 8,
        out_specs=(pl.BlockSpec(memory_space=pltpu.VMEM),) * 2,
        scratch_shapes=scratch,
        compiler_params=pltpu.CompilerParams(collective_id=0, has_side_effects=True),
    )(points, weights, node_proj, skel_idx, near_list, near_count, far_list, far_count)
    return mine + theirs.astype(F32)


def solution(mesh):
    in_specs = (
        P("pts", None), P("pts", None), P(None, "pts"), P("pts", None),
        P("pts", None), P("pts"), P("pts", None), P("pts"),
    )
    return jax.shard_map(shards, mesh=mesh, in_specs=in_specs, out_specs=P("pts", None), check_vma=False)
```

```python
import math

import jax
import jax.numpy as jnp
from jax import lax
from jax.experimental import pallas as pl
from jax.experimental.pallas import tpu as pltpu
from jax.sharding import PartitionSpec as P

F32, BF16 = jnp.float32, jnp.bfloat16
DIM = 1024
SIDE = 4
PTS = 512
COLS = 512
SKL = 32
NODES = 8
LANES = 128
UNIT = 16
SETROWS = SIDE * SKL
SOURCES = SETROWS * SIDE * SIDE
SCALE = math.log2(math.e) * 0.5 / DIM
OFF = -1e38
N_A = {"p": 5, "w": 5}
PIECE = PTS // 4
VIA_X = {"x": (0,), "w": (0, 1, 2, 3)}
NT = (((1,), (1,)), ((), ()))

UNITS = [(0, 0), (0, 1), (0, 3), (0, 2), (1, 2), (1, 3), (1, 1), (1, 0)]
UNIT_AT = {unit: place for place, unit in enumerate(UNITS)}


def body(*refs):
    (x_in, w_in, p_in, idx_in, near_list_in, near_count_in, far_list_in, far_count_in, out1, out2,
     idx, near_list, near_count, far_list, far_count,
     xt, wt, pv, pf, ps, pr, ts, rr, fp, fw, nx, nw, kf, kn, acc, rs, rrecv, hx, hw, early, late, acol, ancol,
     cbo, cbp, cbn, cbf, gate, gatep, stage, lsem, ssem, rsem) = refs
    me = lax.axis_index("pts")
    core = lax.rem(me, 2)
    chip = me // 2
    x, y, z = lax.rem(chip, 4), lax.rem(chip // 4, 4), chip // 16
    sign = 2 * core - 1

    def dev(cx, cy, cz):
        return ((cz * 4 + cy) * 4 + cx) * 2 + core

    def plus(v, d):
        return lax.rem(v + d, 4)

    partner = me + 1 - 2 * core
    xs = {d: dev(plus(x, d), y, z) for d in (1, 3)}
    xfree = jnp.where(core == 0, xs[1], xs[3])
    ys = {d: dev(x, plus(y, d), z) for d in (1, 3)}
    zs = {d: dev(x, y, plus(z, d)) for d in (1, 3)}
    both = jnp.logical_and
    no = jnp.logical_not
    edge = jnp.where(core == 1, 3, 0)
    ahead = {"x": jnp.where(core == 1, xs[1], xs[3]), "y": jnp.where(core == 1, ys[1], ys[3]),
             "z": jnp.where(core == 1, zs[1], zs[3])}
    across = {axis: device - sign for axis, device in ahead.items()}
    xe, ye, ze = x == edge, y == edge, z == edge
    xf, yf, zf = x == 3 - edge, y == 3 - edge, z == 3 - edge
    inner, row_end, plane_end = no(xe), both(xe, no(ye)), both(both(xe, ye), no(ze))
    has_outer = no(both(both(xe, ye), ze))
    ybase = y - lax.rem(y, 2)
    group = {}
    for ry in range(2):
        for rx in range(4):
            if rx or ry:
                cy = lax.rem(lax.rem(y, 2) + ry, 2)
                cx = plus(x, rx)
                group[(rx, ry)] = (dev(cx, ybase + cy, z), cy * 4 + cx)

    loads = []
    for k, (src, dst) in enumerate(((x_in, xt.at[pl.ds(0, PTS)]), (w_in, wt.at[pl.ds(0, PTS)]), (p_in, pv))):
        cp = pltpu.make_async_copy(src, dst, lsem.at[k])
        cp.start()
        loads.append(cp)

    small = []
    for k, (src, dst) in enumerate(((idx_in, idx), (near_list_in, near_list), (near_count_in, near_count),
                                    (far_list_in, far_list), (far_count_in, far_count))):
        cp = pltpu.make_async_copy(src, dst, lsem.at[4 + k])
        cp.start()
        small.append(cp)

    barrier = pltpu.get_barrier_semaphore()
    peers = [d for d, _ in group.values()] + list(ys.values()) + list(zs.values()) + [partner] + list(across.values())
    for d in peers:
        pl.semaphore_signal(barrier, inc=1, device_id=(d,), device_id_type=pl.DeviceIdType.MESH)

    for cp in small:
        cp.wait()

    def any_of(ref, count, value):
        hit = (ref[0, 0] == value) & (count > 0)
        for s in range(1, 4):
            hit = hit | ((ref[0, s] == value) & (count > s))
        return hit

    fcount, ncount = far_count[0], near_count[0]
    for n in range(NODES):
        gate[n : n + 1, :] = jnp.full((1, LANES), jnp.where(any_of(far_list, fcount, n), 0.0, OFF), F32)
    for row, step, found, missing in ((8, 1, 0.0, OFF), (9, -1, 0.0, OFF), (10, 2, 1.0, 0.0), (11, -2, 0.0, OFF)):
        hit = any_of(near_list, ncount, me + sign * step)
        gate[row : row + 1, :] = jnp.full((1, LANES), jnp.where(hit, found, missing), F32)

    rowi = lax.broadcasted_iota(jnp.int32, (SKL, LANES), 0)
    lane = lax.broadcasted_iota(jnp.int32, (SKL, LANES), 1)
    col = jnp.zeros((SKL, LANES), jnp.int32)
    for r in range(SKL):
        col = jnp.where(rowi == r, idx[0, r], col)
    onehot = jnp.concatenate(
        [jnp.where(col == lane + LANES * j, 1.0, 0.0).astype(BF16) for j in range(PTS // LANES)], axis=1
    )
    loads[0].wait()
    skel = jnp.dot(onehot, xt[0:PTS, :], preferred_element_type=F32).astype(BF16)

    def at(dy, dz, unit):
        return (dz * 4 + dy) * SETROWS + unit * UNIT

    for h in range(2):
        fp[pl.ds(at(0, 0, UNIT_AT[(h, 0)]), UNIT), :] = skel[h * UNIT : (h + 1) * UNIT]

    pl.semaphore_wait(barrier, len(peers))

    sent, landing = {}, {}

    started = []

    def send(key, src, dst, device, when=None):
        if key not in landing:
            landing[key] = len(landing)
        cp = pltpu.make_async_remote_copy(
            src_ref=src, dst_ref=dst, send_sem=ssem.at[len(started)], recv_sem=rsem.at[landing[key]],
            device_id=(device,), device_id_type=pl.DeviceIdType.MESH,
        )
        if when is None:
            cp.start()
        else:
            pl.when(when)(cp.start)
        started.append((cp, when))
        sent[key] = cp

    def got(*key):
        sent[key].wait_recv()

    def rows_send(key, buf, device, src, dst, units):
        lo, hi = units
        if hi > lo:
            n = (hi - lo) * UNIT
            send(key, buf.at[pl.ds(at(*src, lo), n)], buf.at[pl.ds(at(*dst, lo), n)], device)

    BUF = {"p": fp, "w": fw}

    def x_own(t):
        for d in (1, 3):
            for h in range(2):
                u, v = UNIT_AT[(h, 0)], UNIT_AT[(h, (4 - d) % 4)]
                send((t, "x", d, h), BUF[t].at[pl.ds(at(0, 0, u), UNIT)], BUF[t].at[pl.ds(at(0, 0, v), UNIT)], xs[d])

    def unit_rows(h, dx):
        return pl.multiple_of(jnp.where(core == 0, UNIT_AT[(h, dx)], UNIT_AT[(h, (4 - dx) % 4)]) * UNIT, UNIT)

    def x_hop(key, t, h, src_dx, dst_dx):
        send(key, BUF[t].at[pl.ds(unit_rows(h, src_dx), UNIT)], BUF[t].at[pl.ds(unit_rows(h, dst_dx), UNIT)], xfree)

    def x_fwd(t):
        for d in (1, 3):
            for h in range(2):
                got(t, "x", d, h)
        for h in range(2):
            x_hop((t, "xf", h), t, h, 3, 2)

    def x_done(t):
        for h in range(2):
            got(t, "xf", h)

    def x_ring(t, step):
        for h in range(2):
            if step:
                got(t, "xr", step - 1, h)
            if step < 3:
                x_hop((t, "xr", step, h), t, h, (4 - step) % 4, 3 - step)

    A_ALL = {t: (0, n) for t, n in N_A.items()}
    B_ALL = {t: (n, 8) for t, n in N_A.items()}
    n_p = N_A["p"]
    GROUPS_A = [(0, 1), (1, 3), (3, n_p)]
    GROUPS_B = [(7, 8), (max(5, n_p), 7), (n_p, max(5, n_p))]

    def piece(ref, k):
        return ref.at[pl.ds(k * PIECE, PIECE)]

    other = {"x": jnp.where(core == 1, xs[3], xs[1]), "y": jnp.where(core == 1, ys[3], ys[1]),
             "z": jnp.where(core == 1, zs[3], zs[1])}
    ENDS = {"x": (xe, ye, ze, xf, yf, zf), "w": (xe, ye, ze, xf, yf, zf)}
    NEXT, FINAL = {"x": ahead, "w": ahead}, {"x": across, "w": across}

    def halo_send(h, ref, pieces, ends=True, inside=True):
        xe, ye, ze, xf, yf, zf = ENDS[h]
        row_end, plane_end, ahead = both(xe, no(ye)), both(both(xe, ye), no(ze)), NEXT[h]
        for k in pieces:
            if inside:
                send((h, "in", k), piece(ref, k), piece(HALO[h], k), across["x"], inner)
            if not ends:
                continue
            axis = "x" if k in VIA_X[h] else "y"
            send((h, "hop", k), piece(ref, k), piece(HOPS[h], k), ahead[axis], row_end)
            axis, slot = (("x", 0), ("x", 1), ("y", 2), ("z", 8))[k]
            send((h, "hop", slot), piece(ref, k), piece(HOPS[h], slot), ahead[axis], plane_end)

    def hop_wait(h, slot, when):
        pl.when(when)(sent[(h, "hop", slot)].wait_recv)

    def hop_send(h, slot, key, axis, when):
        dst = piece(HALO[h], key[2]) if key[1] == "in" else piece(HOPS[h], key[2])
        send(key, piece(HOPS[h], slot), dst, (FINAL if key[1] == "in" else NEXT)[h][axis], when)

    def relay_x(h):
        xe, ye, ze, xf, yf, zf = ENDS[h]
        by_row, by_plane = both(xf, no(ye)), both(both(xf, ye), no(ze))
        for k in range(4):
            here = by_row if k in VIA_X[h] else None
            if k < 2:
                here = by_plane if here is None else here | by_plane
            if here is not None:
                hop_wait(h, k, here)
            if k in VIA_X[h]:
                hop_send(h, k, (h, "in", k), "y", by_row)
        hop_send(h, 0, (h, "hop", 4), "y", by_plane)
        hop_send(h, 1, (h, "hop", 5), "z", by_plane)

    def relay_yz(h):
        xe, ye, ze, xf, yf, zf = ENDS[h]
        by_row, by_plane, by_line = both(xe, no(yf)), both(both(xe, yf), no(ze)), both(both(xe, ye), no(zf))
        for k in range(4):
            here = None if k in VIA_X[h] else by_row
            if k == 2:
                here = by_plane if here is None else here | by_plane
            if here is not None:
                hop_wait(h, k, here)
            if k not in VIA_X[h]:
                hop_send(h, k, (h, "in", k), "x", by_row)
        hop_send(h, 2, (h, "hop", 6), "z", by_plane)
        hop_wait(h, 8, by_line)
        hop_send(h, 8, (h, "hop", 7), "y", by_line)

    def relay_last(h):
        xe, ye, ze, xf, yf, zf = ENDS[h]
        for slot, k, axis, when in (
            (4, 0, "z", both(both(xf, yf), no(ze))),
            (5, 1, "y", both(both(xf, ye), no(zf))),
            (6, 2, "x", both(both(xe, yf), no(zf))),
            (7, 3, "x", both(both(xe, yf), no(zf))),
        ):
            hop_wait(h, slot, when)
            hop_send(h, slot, (h, "in", k), axis, when)

    def halo_got(h):
        for k in range(4):
            pl.when(has_outer)(sent[(h, "in", k)].wait_recv)

    HALO = {"x": nx, "w": nw}
    HOPS = {"x": hx, "w": hw}

    y_even = lax.rem(y, 2) == 0
    y_far, y_pair = jnp.where(y_even, ys[3], ys[1]), jnp.where(y_even, ys[1], ys[3])
    y_seen, y_from = jnp.where(y_even, 1, 3), jnp.where(y_even, 3, 1)
    near_base = jnp.where(y_even, 2, 1)
    near_rows = pl.multiple_of(near_base * SETROWS, SETROWS)

    def pass_same(key, t, device, src, dst, units):
        lo, hi = units
        if hi > lo:
            n = (hi - lo) * UNIT
            src, dst = (
                pl.multiple_of(slot * SETROWS + lo * UNIT, UNIT) if not isinstance(slot, int) else slot * SETROWS + lo * UNIT
                for slot in (src, dst)
            )
            send(key, BUF[t].at[pl.ds(src, n)], BUF[t].at[pl.ds(dst, n)], device)

    def stage_one(t, ga, gb, tag):
        for d in (1, 3):
            rows_send((t, "A2", d, tag), BUF[t], ys[d], (0, 0), ((4 - d) % 4, 0), ga)
            rows_send((t, "B2", d, tag), BUF[t], zs[d], (0, 0), (0, (4 - d) % 4), gb)
        for d in (1, 3):
            rows_send((t, "A3", d, 0, tag), BUF[t], zs[d], (0, 0), (0, (4 - d) % 4), ga)
        pass_same((t, "B0", 0, tag), t, y_far, 0, y_seen, gb)

    def wait_all(t, kind, d, *more):
        for key in list(sent):
            if key[:3] == (t, kind, d) and key[3 : 3 + len(more)] == more:
                got(*key)

    def cut(units, flip):
        lo, hi = units
        mid = lo + (hi - lo + (0 if flip else 1)) // 2
        return (lo, mid), (mid, hi)

    def pass_on(key, t, axis, other, units):
        for part, (lo, hi) in enumerate(units):
            if hi <= lo:
                continue
            slot, d = ((3, 1), (1, 3))[part]
            if axis == "y":
                rows_send(key + (part,), BUF[t], ys[d], (slot, other), (2, other), (lo, hi))
            else:
                rows_send(key + (part,), BUF[t], zs[d], (other, slot), (other, 2), (lo, hi))

    def leg_two(t):
        for d in (1, 3):
            wait_all(t, "A2", d)
        pass_on((t, "A2f", 0), t, "y", 0, cut(A_ALL[t], False))
        for d in (1, 3):
            wait_all(t, "B2", d)
        pass_on((t, "B2f", 0), t, "z", 0, cut(B_ALL[t], False))
        for s in (3, 1):
            for d in (1, 3):
                rows_send((t, "A3", d, s), BUF[t], zs[d], (s, 0), (s, (4 - d) % 4), A_ALL[t])
                rows_send((t, "B3", d, s), BUF[t], ys[d], (0, s), ((4 - d) % 4, s), B_ALL[t])

    def leg_far(t):
        wait_all(t, "A2f", 0)
        wait_all(t, "B2f", 0)
        for d in (1, 3):
            rows_send((t, "A3", d, 2), BUF[t], zs[d], (2, 0), (2, (4 - d) % 4), A_ALL[t])
            rows_send((t, "B3", d, 2), BUF[t], ys[d], (0, 2), ((4 - d) % 4, 2), B_ALL[t])

    def last_fwd(t, s):
        for d in (1, 3):
            wait_all(t, "A3", d, s)
        pass_on((t, "A3f", s), t, "z", s, cut(A_ALL[t], s % 2 == 1))
        if s == 0:
            wait_all(t, "B0", 0)
            pass_same((t, "B3f", 0, 0), t, y_pair, y_from, 2, B_ALL[t])
            return
        for d in (1, 3):
            wait_all(t, "B3", d, s)
        pass_on((t, "B3f", s), t, "y", s, cut(B_ALL[t], s % 2 == 1))

    def last_done(t, kind, s):
        wait_all(t, kind, s)

    def sq_rows(ref, r0, out, o0, n):
        @pl.loop(0, n)
        def _(i):
            v = ref[pl.ds(pl.multiple_of(r0 + i * LANES, LANES), LANES), :].astype(F32)
            v = v * v
            t = v[:, 0:LANES]
            for j in range(1, DIM // LANES):
                t = t + v[:, j * LANES : (j + 1) * LANES]
            out[pl.ds(o0 + i, 1), :] = jnp.sum(t.T, axis=0, keepdims=True) * (-SCALE)

    def sq_cols(ref, r0, out, n):
        @pl.loop(0, n)
        def _(i):
            at_row = pl.multiple_of(r0 + i * LANES, LANES)
            v = ref[pl.ds(at_row, LANES), :].astype(F32)
            t = jnp.sum(v * v, axis=1, keepdims=True) * (-SCALE)
            out[pl.ds(at_row, LANES), :] = jnp.broadcast_to(t, (LANES, LANES))

    def kern_tile(xref, x0, colref, yref, y0, bias, kout, k0, n=PTS):
        s = lax.dot_general(xref[pl.ds(x0, PTS), :], yref[pl.ds(y0, n), :], NT, preferred_element_type=F32)
        a = colref[pl.ds(x0, PTS), :]
        for j in range(n // LANES):
            e = s[:, j * LANES : (j + 1) * LANES] * (2.0 * SCALE) + (a + bias(j))
            kout[pl.ds(x0, PTS), k0 + j * LANES : k0 + (j + 1) * LANES] = jnp.exp2(e).astype(BF16)

    x_own("p")
    stage_one("p", GROUPS_A[0], GROUPS_B[0], 0)
    send(("x",), x_in, xt.at[pl.ds(PTS, PTS)], partner)
    halo_send("x", x_in, (0, 1))
    halo_send("x", x_in, (2,), inside=False)
    send(("w",), w_in, wt.at[pl.ds(PTS, PTS)], partner)
    send(("g",), gate, gatep, partner)

    loads[1].wait()
    loads[2].wait()
    pf[...] = jnp.dot(pv[...], wt[0:PTS, :], preferred_element_type=F32)
    for j in range(NODES):
        ps[pl.ds(j * SKL, SKL), :] = pf[pl.ds(pl.multiple_of(64 * j + 32 * (1 - core), 32), SKL), :].astype(BF16)
    sq_rows(xt, 0, cbo, 0, 4)
    send(("ps",), ps, pr, partner)

    x_fwd("p")
    stage_one("p", GROUPS_A[1], GROUPS_B[1], 1)
    sq_cols(xt, 0, acol, 4)

    got("ps")
    for j in range(NODES):
        mine = pf[pl.ds(pl.multiple_of(64 * j + 32 * core, 32), SKL), :] + pr[pl.ds(j * SKL, SKL), :].astype(F32)
        ts[pl.ds(j * SKL, SKL), :] = mine.astype(BF16)
    x_done("p")
    stage_one("p", GROUPS_A[2], GROUPS_B[2], 2)
    for (rx, ry), (device, j) in group.items():
        slot = ry * 4 + rx
        send(("rs", slot), ts.at[pl.ds(pl.multiple_of(j * SKL, SKL), SKL)], rr.at[pl.ds(slot * SKL, SKL)], device)
    halo_send("x", x_in, (2,), ends=False)
    halo_send("x", x_in, (3,))

    def own_task(leaf):
        def bias(j):
            row = cbo[j : j + 1, :]
            return row if leaf == 0 else row + gatep[9:10, :]

        kern_tile(xt, leaf * PTS, acol, xt, 0, bias, kn, 0)
        rows = slice(leaf * PTS, (leaf + 1) * PTS)
        acc[rows, :] = jnp.dot(kn[rows, :], wt[0:PTS, :], preferred_element_type=F32)

    own_task(0)
    leg_two("p")
    relay_x("x")

    own_row = pl.multiple_of((lax.rem(y, 2) * 4 + x) * 64 + 32 * core, 32)
    own_j = pl.multiple_of((lax.rem(y, 2) * 4 + x) * SKL, 32)
    block = pf[pl.ds(own_row, SKL), :] + pr[pl.ds(own_j, SKL), :].astype(F32)
    for slot in range(1, NODES):
        got("rs", slot)
        block = block + rr[pl.ds(slot * SKL, SKL), :].astype(F32)
    block = block.astype(BF16)
    for h in range(2):
        fw[pl.ds(at(0, 0, UNIT_AT[(h, 0)]), UNIT), :] = block[h * UNIT : (h + 1) * UNIT]
    got("x")
    sq_cols(xt, PTS, acol, 4)
    x_ring("w", 0)
    sq_rows(xt, PTS, cbp, 0, 4)
    last_fwd("p", 0)
    x_ring("w", 1)
    halo_send("w", w_in, (0, 1, 2, 3), inside=False)
    halo_send("w", w_in, (0, 1, 2, 3), ends=False)
    got("g")
    own_task(1)
    x_ring("w", 2)
    got("w")
    leg_far("p")
    relay_yz("x")
    x_ring("w", 3)
    stage_one("w", A_ALL["w"], B_ALL["w"], 0)
    last_fwd("p", 3)
    last_fwd("p", 1)
    relay_last("x")

    def far_kern(g):
        sets, first, base = (4, g * PTS, 0) if g else (2, near_rows, near_base)
        sq_rows(fp, first, cbf, 4 * g, sets)
        for dy in range(sets):
            node = plus(z, g) * 2 + plus(y, base + dy) // 2
            s = 4 * g + dy
            row = cbf[s : s + 1, :]
            stage[s : s + 1, :] = row + gate[pl.ds(node, 1), :]
            stage[16 + s : 17 + s, :] = row + gatep[pl.ds(node, 1), :]

        @pl.loop(0, 2)
        def _(leaf):
            def bias(j):
                return stage[pl.ds(leaf * 16 + 4 * g + j, 1), :]

            kern_tile(xt, pl.multiple_of(leaf * PTS, PTS), acol, fp, first, bias, kf, g * PTS, sets * SETROWS)

    last_done("p", "B3f", 0)
    far_kern(0)
    relay_x("w")
    leg_two("w")
    last_fwd("p", 2)
    relay_yz("w")
    last_fwd("w", 0)

    halo_got("x")

    @pl.when(has_outer)
    def _():
        sq_rows(nx, 0, cbn, 0, 4)
        sq_cols(nx, 0, ancol, 4)
        kern_tile(nx, 0, ancol, xt, PTS, lambda j: cbp[j : j + 1, :], kn, 0)
        rs[...] = jnp.dot(kn[0:PTS, :], wt[PTS : 2 * PTS, :], preferred_element_type=F32).astype(BF16)

    send(("r",), rs, rrecv, jnp.where(has_outer, me + sign, me), has_outer)

    for s in (1, 3):
        last_done("p", "B3f", s)
    far_kern(3)
    leg_far("w")
    relay_last("w")
    far_kern(1)
    last_fwd("w", 3)
    last_fwd("w", 1)

    @pl.when(has_outer)
    def _():
        for leaf, row, ref in ((0, 8, gate), (1, 11, gatep)):
            kern_tile(xt, leaf * PTS, acol, nx, 0, lambda j: cbn[j : j + 1, :] + ref[row : row + 1, :], kn, 0)

    last_done("p", "B3f", 2)
    for s in range(4):
        last_done("p", "A3f", s)
    far_kern(2)
    last_fwd("w", 2)

    def far_product(g, leaf):
        first, n = (g * PTS, PTS) if g else (near_rows, 2 * SETROWS)
        return jnp.dot(
            kf[leaf * PTS : (leaf + 1) * PTS, g * PTS : g * PTS + n], fw[pl.ds(first, n), :],
            preferred_element_type=F32,
        )

    def far_sum(g, leaf):
        acc[leaf * PTS : (leaf + 1) * PTS, :] += far_product(g, leaf)

    last_done("w", "B3f", 0)
    for leaf in (1, 0):
        far_sum(0, leaf)
    halo_got("w")

    @pl.when(has_outer)
    def _():
        for leaf in range(2):
            rows = slice(leaf * PTS, (leaf + 1) * PTS)
            acc[rows, :] += jnp.dot(kn[rows, :], nw[...], preferred_element_type=F32)

    last_done("w", "B3f", 3)
    last_done("w", "B3f", 1)
    for leaf in (1, 0):
        for g in (3, 1):
            far_sum(g, leaf)
    send(("acc",), acc.at[pl.ds(PTS, PTS)], early, partner)

    @pl.when(has_outer)
    def _():
        got("r")
        for j in range(COLS // LANES):
            c = slice(j * LANES, (j + 1) * LANES)
            acc[0:PTS, c] = acc[0:PTS, c] + rrecv[:, c].astype(F32) * gate[10:11, :]

    last_done("w", "B3f", 2)
    for s in range(4):
        last_done("w", "A3f", s)
    late[...] = far_product(2, 1).astype(BF16)
    got("acc")
    acc[0:PTS, :] += early[...]
    send(("late",), late, out2, partner)
    out1[...] = acc[0:PTS, :] + far_product(2, 0)
    got("late")
    for copy, when in started:
        if when is None:
            copy.wait_send()
        else:
            pl.when(when)(copy.wait_send)


def shards(points, weights, node_proj, skel_idx, near_list, near_count, far_list, far_count):
    hbm = pl.BlockSpec(memory_space=pl.ANY)
    vm = pltpu.VMEM
    words = [pltpu.SMEM(a.shape, a.dtype) for a in (skel_idx, near_list, near_count, far_list, far_count)]
    scratch = words + [
        vm((2 * PTS, DIM), BF16), vm((2 * PTS, COLS), BF16), vm((PTS, PTS), BF16), vm((PTS, COLS), F32),
        vm((NODES * SKL, COLS), BF16), vm((NODES * SKL, COLS), BF16), vm((NODES * SKL, COLS), BF16),
        vm((NODES * SKL, COLS), BF16),
        vm((SOURCES, DIM), BF16), vm((SOURCES, COLS), BF16), vm((PTS, DIM), BF16), vm((PTS, COLS), BF16),
        vm((2 * PTS, SOURCES), BF16), vm((2 * PTS, PTS), BF16), vm((2 * PTS, COLS), F32),
        vm((PTS, COLS), BF16), vm((PTS, COLS), BF16),
        vm((9 * PIECE, DIM), BF16), vm((9 * PIECE, COLS), BF16),
        vm((PTS, COLS), F32), vm((PTS, COLS), BF16),
        vm((2 * PTS, LANES), F32), vm((PTS, LANES), F32),
        vm((8, LANES), F32), vm((8, LANES), F32), vm((8, LANES), F32), vm((16, LANES), F32),
        vm((16, LANES), F32), vm((16, LANES), F32), vm((32, LANES), F32),
        pltpu.SemaphoreType.DMA((9,)), pltpu.SemaphoreType.DMA((240,)), pltpu.SemaphoreType.DMA((200,)),
    ]
    mine, theirs = pl.pallas_call(
        body,
        out_shape=(pltpu.VMEM((PTS, COLS), F32), pltpu.VMEM((PTS, COLS), BF16)),
        in_specs=[hbm] * 8,
        out_specs=(pl.BlockSpec(memory_space=pltpu.VMEM),) * 2,
        scratch_shapes=scratch,
        compiler_params=pltpu.CompilerParams(collective_id=0, has_side_effects=True),
    )(points, weights, node_proj, skel_idx, near_list, near_count, far_list, far_count)
    return mine + theirs.astype(F32)


def solution(mesh):
    in_specs = (
        P("pts", None), P("pts", None), P(None, "pts"), P("pts", None),
        P("pts", None), P("pts"), P("pts", None), P("pts"),
    )
    return jax.shard_map(shards, mesh=mesh, in_specs=in_specs, out_specs=P("pts", None), check_vma=False)
```
